32 devices in a mesh: groups: 2 (over x), pool: 2 (over core), tensor: 8 (over z, y).
Axes of the slice: x: 2, y: 2, z: 4, core: 2. Of those that a mesh axis runs over, the one named last changes fastest.
Arguments:
- hidden: bfloat16 [64, 5120], P(('groups', 'pool', 'tensor')), parts along dimension 0, may hold values from -1.5 to 1.5
- input_gain: float32 [5120], replicated, may hold values from 0.1 to 1.9
- query_weight: bfloat16 [5120, 4096], P(None, ('pool', 'tensor')), may hold values from -0.078125 to 0.078125
- key_weight: bfloat16 [5120, 512], P(None, ('pool', 'tensor')), may hold values from -0.078125 to 0.078125
- value_weight: bfloat16 [5120, 512], P(None, ('pool', 'tensor')), may hold values from -0.078125 to 0.078125
- query_gain: float32 [128], replicated, may hold values from 2 to 6
- key_gain: float32 [128], replicated, may hold values from 1 to 4
- output_weight: bfloat16 [4096, 5120], P(('pool', 'tensor')), may hold values from -0.09375 to 0.09375
- post_gain: float32 [5120], replicated, may hold values from 0.1 to 1.9
- gate_weight: bfloat16 [5120, 12800], P(None, ('pool', 'tensor')), may hold values from -0.078125 to 0.078125
- up_weight: bfloat16 [5120, 12800], P(None, ('pool', 'tensor')), may hold values from -0.078125 to 0.078125
- down_weight: bfloat16 [12800, 5120], P(('pool', 'tensor')), may hold values from -0.0546875 to 0.0546875
- key_cache: bfloat16 [65536, 512], P(('groups', 'pool', 'tensor')), parts along dimension 0, may hold values from -45 to 45
- value_cache: bfloat16 [65536, 512], P(('groups', 'pool', 'tensor')), parts along dimension 0, may hold values from -6 to 6
- lengths: int32 [64], P('groups'), parts along dimension 0, may hold values from 128 to 2048, as said below
- request_slot: int32 [64], P('groups'), parts along dimension 0, may hold values from 0 to 63, as said below
Outputs:
- mixed: bfloat16 [64, 5120], P(('groups', 'pool', 'tensor')), parts along dimension 0
- final: bfloat16 [64, 5120], P(('groups', 'pool', 'tensor')), parts along dimension 0
The draws below stay inside these ranges and needn't reach their ends.
There are 2 independent parts, one for each index of `groups`. The reference program is written for one: setup_inputs(seed, part) draws one part's arguments, and reference() takes and returns one part's arrays. A program takes and returns all parts, laid end to end along the dimension named above; an argument that names none is the same for every part. Nothing has to cross between parts.
Inputs may be any that keep to these rules, and one draw needn't show every extreme that they name: `request_slot`: each owner holds at most 4 requests and some owner holds exactly 4; no two requests share a slot. The lengths of one owner's requests sum to at most 2048; some request has exactly 2048 and some exactly 128.
All inputs are finite; a program needn't handle non-finite values.
Results may differ from the reference program's by a relative error of at most 0.03.
The reference program's roundings to bfloat16 on the way count: a program that leaves them out, or rounds other values in their place, can miss the bound.
Values may be sent and summed in bfloat16 or wider, within the bound.
A program may use at most 64 MiB of HBM per device.

```python
import math
import jax
import jax.numpy as jnp
from jax import lax

D = 5120
HEADS = 32
KV_HEADS = 4
HD = 128
FF = 12800
SLOTS = 4
MAXLEN = 2048
MINLEN = 128
OWNERS = 16
REQ = 32
QD = 4096
KD = 512


def request_layout(key):
    folded = jax.random.fold_in(key, 7)
    key_owner, key_length, key_order = jax.random.split(folded, 3)
    pattern = jnp.tile(jnp.array([4, 1, 2, 1], jnp.int32), OWNERS // 4)
    owner_order = jax.random.permutation(key_owner, OWNERS)
    counts = jnp.zeros((OWNERS,), jnp.int32).at[owner_order].set(pattern)
    slot_ids = jnp.arange(OWNERS * SLOTS, dtype=jnp.int32)
    usable = slot_ids % SLOTS < counts[slot_ids // SLOTS]
    ranked = jnp.sort(jnp.where(usable, slot_ids, slot_ids + OWNERS * SLOTS))[:REQ]
    chosen = ranked[jax.random.permutation(key_order, REQ)]
    holders = counts[chosen // SLOTS]
    ceiling = MAXLEN // holders
    length_draw = jax.random.randint(key_length, (REQ,), MINLEN, ceiling + 1)
    length_draw = jnp.where(chosen == owner_order[1] * SLOTS, MAXLEN, length_draw)
    length_draw = jnp.where(chosen == owner_order[0] * SLOTS, MINLEN, length_draw)
    return (chosen.astype(jnp.int32), length_draw.astype(jnp.int32))


def draw_request_slot(key, part):
    return request_layout(key)[0]


def draw_lengths(key, part):
    return request_layout(key)[1]


def draw_key_cache(key, part):
    row_total = OWNERS * MAXLEN
    drawn = jnp.clip(jax.random.normal(jax.random.fold_in(key, 13), (row_total, KV_HEADS * HD), jnp.float32), -6.0, 6.0)
    return drawn.astype(jnp.bfloat16)


def level_of(key, extent, cuts, least, top_value):
    level, own = 1.0, jax.random.fold_in(key, 6)
    for dim, shards_of in cuts:
        steps = jnp.exp(jax.random.uniform(jax.random.fold_in(own, dim), (shards_of,), jnp.float32, least / len(cuts), top_value / len(cuts)))
        level = level * jnp.repeat(steps, extent[dim] // shards_of).reshape([-1 if axis == dim else 1 for axis in range(len(extent))])
    return level


def scatter_about(key, dims, deviation, limit, pieces=(), kind=jnp.bfloat16):
    result = deviation * jax.random.normal(key, dims, jnp.float32)
    if pieces:
        result = result * level_of(key, dims, pieces, -0.22, 0.18)
    return jnp.clip(result, -limit, limit).astype(kind)


def setup_inputs(seed: int = 0, part: int = 0) -> dict:
    splits = jax.random.split(jax.random.key(seed), 17)
    part_splits = jax.random.split(jax.random.fold_in(splits[16], part), 17)
    return {
        "hidden": scatter_about(part_splits[0], (REQ, D), 0.25, 1.5, ((0, 16),)),
        "input_gain": jnp.clip(1.0 + 0.18 * jax.random.normal(splits[1], (D,), jnp.float32), 0.1, 1.9),
        "query_weight": scatter_about(splits[2], (D, QD), D ** -0.5, 0.078125, ((1, 16),)),
        "key_weight": scatter_about(splits[3], (D, KD), D ** -0.5, 0.078125, ((1, 16),)),
        "value_weight": scatter_about(splits[4], (D, KD), D ** -0.5, 0.078125, ((1, 16),)),
        "query_gain": jnp.clip(jnp.exp(jax.random.uniform(splits[5], (HD,), jnp.float32, math.log(2.0), math.log(6.0))), 2.0, 6.0),
        "key_gain": jnp.clip(jnp.exp(jax.random.uniform(splits[6], (HD,), jnp.float32, math.log(1.0), math.log(4.0))), 1.0, 4.0),
        "output_weight": scatter_about(splits[7], (QD, D), QD ** -0.5, 0.09375, ((0, 16),)),
        "post_gain": jnp.clip(1.0 + 0.18 * jax.random.normal(splits[8], (D,), jnp.float32), 0.1, 1.9),
        "gate_weight": scatter_about(splits[9], (D, FF), D ** -0.5, 0.078125, ((1, 16),)),
        "up_weight": scatter_about(splits[10], (D, FF), D ** -0.5, 0.078125, ((1, 16),)),
        "down_weight": scatter_about(splits[11], (FF, D), FF ** -0.5, 0.0546875, ((0, 16),)),
        "key_cache": draw_key_cache(jax.random.fold_in(jax.random.fold_in(splits[16], part), 71), part),
        "value_cache": scatter_about(part_splits[13], (OWNERS * MAXLEN, KD), 1.0, 6.0, ((0, 16),)),
        "lengths": draw_lengths(jax.random.fold_in(jax.random.fold_in(splits[16], part), 71), part),
        "request_slot": draw_request_slot(jax.random.fold_in(jax.random.fold_in(splits[16], part), 71), part),
    }


eps = 1e-06
theta = 1000000.0

def rms_scale(values, scales):
    values = values.astype(jnp.float32)
    return values * lax.rsqrt(lax.optimization_barrier(jnp.mean(values * values, axis=-1, keepdims=True)) + eps) * scales

def rotate(values, position):
    half_width = values.shape[-1] // 2
    frequency = theta ** (-jnp.arange(half_width, dtype=jnp.float32) * 2.0 / values.shape[-1])
    angles = position * frequency
    cosine = jnp.cos(angles)
    sine_part = jnp.sin(angles)
    front_half = values[..., :half_width]
    back_half = values[..., half_width:]
    return jnp.concatenate([front_half * cosine - back_half * sine_part, back_half * cosine + front_half * sine_part], axis=-1)

def reference(hidden, input_gain, query_weight, key_weight, value_weight, query_gain, key_gain, output_weight, post_gain, gate_weight, up_weight, down_weight, key_cache, value_cache, lengths, request_slot):
    requests = hidden.shape[0]
    group_size = HEADS // KV_HEADS
    normed = rms_scale(hidden, input_gain).astype(jnp.bfloat16)
    query_rows = jnp.dot(normed, query_weight, preferred_element_type=jnp.float32).astype(jnp.bfloat16)
    key_rows = jnp.dot(normed, key_weight, preferred_element_type=jnp.float32).astype(jnp.bfloat16)
    value_rows = jnp.dot(normed, value_weight, preferred_element_type=jnp.float32).astype(jnp.bfloat16)
    position = lengths.astype(jnp.float32)[:, None, None]
    query_heads = rotate(rms_scale(query_rows.reshape(requests, HEADS, HD), query_gain), position).astype(jnp.bfloat16)
    query_heads = query_heads.reshape(requests, KV_HEADS, group_size, HD)
    key_new = rotate(rms_scale(key_rows.reshape(requests, KV_HEADS, HD), key_gain), position).astype(jnp.bfloat16)
    value_new = value_rows.reshape(requests, KV_HEADS, HD)
    owner_of = (request_slot // SLOTS).astype(jnp.int32)
    within = request_slot % SLOTS
    earlier = (owner_of[None, :] == owner_of[:, None]) & (within[None, :] < within[:, None])
    offsets = lax.optimization_barrier(jnp.sum(jnp.where(earlier, lengths[None, :], 0), axis=1)).astype(jnp.int32)
    pooled_keys = key_cache.reshape(OWNERS, MAXLEN, KV_HEADS, HD)
    pooled_values = value_cache.reshape(OWNERS, MAXLEN, KV_HEADS, HD)
    token_pos = jnp.arange(MAXLEN, dtype=jnp.int32)
    scale_factor = 1.0 / math.sqrt(HD)

    def attend(items):
        query_one, key_one, value_one, owner_one, offset_one, length_one = items
        keys_here = lax.dynamic_index_in_dim(pooled_keys, owner_one, 0, keepdims=False).astype(jnp.float32)
        values_here = lax.dynamic_index_in_dim(pooled_values, owner_one, 0, keepdims=False).astype(jnp.float32)
        query_float = query_one.astype(jnp.float32)
        scores = jnp.einsum('kgd,tkd->kgt', query_float, keys_here) * scale_factor
        own_score = jnp.einsum('kgd,kd->kg', query_float, key_one.astype(jnp.float32)) * scale_factor
        inside = ((token_pos >= offset_one) & (token_pos < offset_one + length_one))[None, None, :]
        largest = jnp.maximum(lax.optimization_barrier(jnp.max(jnp.where(inside, scores, -1e+30), axis=2)), own_score)
        weights = jnp.where(inside, jnp.exp(scores - largest[..., None]), 0.0)
        own_weight = jnp.exp(own_score - largest)
        denominator = lax.optimization_barrier(jnp.sum(weights, axis=2)) + own_weight
        weights_low = weights.astype(jnp.bfloat16).astype(jnp.float32)
        own_low = own_weight.astype(jnp.bfloat16).astype(jnp.float32)
        summed = jnp.einsum('kgt,tkd->kgd', weights_low, values_here)
        summed = summed + own_low[..., None] * value_one.astype(jnp.float32)[:, None, :]
        return (summed / denominator[..., None]).astype(jnp.bfloat16).reshape(HEADS * HD)
    head_rows = lax.map(attend, (query_heads, key_new, value_new, owner_of, offsets, lengths.astype(jnp.int32)))
    attended = jnp.dot(head_rows, output_weight, preferred_element_type=jnp.float32)
    mixed = (hidden.astype(jnp.float32) + attended).astype(jnp.bfloat16)
    post_normed = rms_scale(mixed, post_gain).astype(jnp.bfloat16)
    gate_part = jnp.dot(post_normed, gate_weight, preferred_element_type=jnp.float32)
    up_part = jnp.dot(post_normed, up_weight, preferred_element_type=jnp.float32)
    activated = (jax.nn.silu(gate_part) * up_part).astype(jnp.bfloat16)
    lowered = jnp.dot(activated, down_weight, preferred_element_type=jnp.float32)
    final = (mixed.astype(jnp.float32) + lowered).astype(jnp.bfloat16)
    return (mixed, final)
```

```python
import functools
import math

import jax
import jax.numpy as jnp
import numpy as np
from jax import lax
from jax.experimental import pallas as pl
from jax.experimental.pallas import tpu as pltpu
from jax.sharding import PartitionSpec as P

SLOTS = 4


eps = 1e-06
theta = 1000000.0


def rms_scale(values, scales):
    values = values.astype(jnp.float32)
    return values * lax.rsqrt(jnp.mean(values * values, axis=-1, keepdims=True) + eps) * scales


def rotate(values, position):
    half_width = values.shape[-1] // 2
    frequency = theta ** (-jnp.arange(half_width, dtype=jnp.float32) * 2.0 / values.shape[-1])
    angles = position * frequency
    cosine = jnp.cos(angles)
    sine_part = jnp.sin(angles)
    front_half = values[..., :half_width]
    back_half = values[..., half_width:]
    return jnp.concatenate(
        [front_half * cosine - back_half * sine_part, back_half * cosine + front_half * sine_part],
        axis=-1,
    )


def on_device(
    hidden,
    input_gain,
    query_weight,
    key_weight,
    value_weight,
    query_gain,
    key_gain,
    output_weight,
    post_gain,
    gate_weight,
    up_weight,
    down_weight,
    key_cache,
    value_cache,
    lengths,
    request_slot,
):
    devices = lax.axis_size(("pool", "tensor"))
    device_index = lax.axis_index(("pool", "tensor"))
    local_rows = hidden.shape[0]
    query_cols = query_weight.shape[1]
    key_cols = key_weight.shape[1]
    width_sent = query_cols + 2 * key_cols
    head_dim = query_gain.shape[0]
    slot_count = SLOTS
    head_count = devices * query_cols // head_dim
    kv_count = devices * key_cols // head_dim
    group_size = head_count // kv_count
    normed = rms_scale(hidden, input_gain).astype(jnp.bfloat16)
    shard_rows = lax.all_gather(normed, ("pool", "tensor"), axis=0, tiled=True)
    query_part = jnp.dot(shard_rows, query_weight, preferred_element_type=jnp.float32)
    key_part = jnp.dot(shard_rows, key_weight, preferred_element_type=jnp.float32)
    value_part = jnp.dot(shard_rows, value_weight, preferred_element_type=jnp.float32)
    projected = jnp.concatenate([query_part, key_part, value_part], axis=1).astype(jnp.bfloat16)
    outgoing = (
        jnp.zeros((devices * slot_count, width_sent), jnp.bfloat16).at[request_slot].set(projected)
    )
    outgoing = outgoing.reshape(devices, slot_count, width_sent)
    arrived = lax.all_to_all(
        outgoing, ("pool", "tensor"), split_axis=0, concat_axis=2, tiled=True
    ).reshape(slot_count, devices, width_sent)
    query_full = arrived[:, :, :query_cols].reshape(slot_count, head_count, head_dim)
    key_full = arrived[:, :, query_cols : query_cols + key_cols].reshape(
        slot_count, kv_count, head_dim
    )
    value_new = arrived[:, :, query_cols + key_cols :].reshape(slot_count, kv_count, head_dim)
    slot_ids = device_index * slot_count + jnp.arange(slot_count, dtype=jnp.int32)
    matches = request_slot[None, :] == slot_ids[:, None]
    slot_length = jnp.sum(jnp.where(matches, lengths[None, :], 0), axis=1)
    owner_of = request_slot // slot_count
    within = request_slot % slot_count
    earlier = (owner_of[None, :] == device_index) & (
        within[None, :] < jnp.arange(slot_count, dtype=jnp.int32)[:, None]
    )
    slot_offset = jnp.sum(jnp.where(earlier, lengths[None, :], 0), axis=1)
    position = slot_length.astype(jnp.float32)[:, None, None]
    query_heads = rotate(rms_scale(query_full, query_gain), position).astype(jnp.bfloat16)
    query_heads = query_heads.reshape(slot_count, kv_count, group_size, head_dim)
    key_new = rotate(rms_scale(key_full, key_gain), position).astype(jnp.bfloat16)
    pool_tokens = key_cache.shape[0]
    cached_keys = key_cache.reshape(pool_tokens, kv_count, head_dim)
    cached_values = value_cache.reshape(pool_tokens, kv_count, head_dim)
    scale_factor = 1.0 / math.sqrt(head_dim)
    scores = (
        jnp.einsum("skgd,tkd->skgt", query_heads, cached_keys, preferred_element_type=jnp.float32)
        * scale_factor
    )
    own_score = (
        jnp.einsum("skgd,skd->skg", query_heads, key_new, preferred_element_type=jnp.float32)
        * scale_factor
    )
    token_pos = jnp.arange(pool_tokens, dtype=jnp.int32)
    inside = (token_pos[None, :] >= slot_offset[:, None]) & (
        token_pos[None, :] < (slot_offset + slot_length)[:, None]
    )
    inside = inside[:, None, None, :]
    largest = jnp.maximum(jnp.max(jnp.where(inside, scores, -1e30), axis=3), own_score)
    weights = jnp.where(inside, jnp.exp(scores - largest[..., None]), 0.0)
    own_weight = jnp.exp(own_score - largest)
    denominator = jnp.sum(weights, axis=3) + own_weight
    summed = jnp.einsum(
        "skgt,tkd->skgd",
        weights.astype(jnp.bfloat16),
        cached_values,
        preferred_element_type=jnp.float32,
    )
    own_low = own_weight.astype(jnp.bfloat16).astype(jnp.float32)
    summed = summed + own_low[..., None] * value_new.astype(jnp.float32)[:, :, None, :]
    head_out = (
        (summed / denominator[..., None])
        .astype(jnp.bfloat16)
        .reshape(slot_count, devices, query_cols)
    )
    returned = lax.all_to_all(head_out, ("pool", "tensor"), split_axis=1, concat_axis=0, tiled=True)
    head_rows = returned.reshape(devices * slot_count, query_cols)[request_slot]
    partial_value = jnp.dot(head_rows, output_weight, preferred_element_type=jnp.float32)
    row_start = device_index * local_rows
    own_part = lax.dynamic_slice_in_dim(partial_value, row_start, local_rows, 0) + hidden.astype(
        jnp.float32
    )
    partial_value = lax.dynamic_update_slice_in_dim(partial_value, own_part, row_start, 0)
    totals = lax.psum(partial_value, ("pool", "tensor"))
    mixed_all = totals.astype(jnp.bfloat16)
    mixed_rows = lax.dynamic_slice_in_dim(mixed_all, row_start, local_rows, 0)
    post_normed = rms_scale(mixed_all, post_gain).astype(jnp.bfloat16)
    gate_part = jnp.dot(post_normed, gate_weight, preferred_element_type=jnp.float32)
    up_part = jnp.dot(post_normed, up_weight, preferred_element_type=jnp.float32)
    activated = (jax.nn.silu(gate_part) * up_part).astype(jnp.bfloat16)
    lowered = lax.psum_scatter(
        jnp.dot(activated, down_weight, preferred_element_type=jnp.float32),
        ("pool", "tensor"),
        scatter_dimension=0,
        tiled=True,
    )
    final_rows = (mixed_rows.astype(jnp.float32) + lowered).astype(jnp.bfloat16)
    return (mixed_rows, final_rows)


MESH = pl.DeviceIdType.MESH
F32 = jnp.float32
BF16 = jnp.bfloat16


def step_kernel(
    pool,
    tensor,
    hidden_ref,
    input_gain_ref,
    query_gain_ref,
    key_gain_ref,
    post_gain_ref,
    length_ref,
    slot_ref,
    frequency_ref,
    qw_hbm,
    kw_hbm,
    vw_hbm,
    ow_hbm,
    gw_hbm,
    uw_hbm,
    dw_hbm,
    kc_hbm,
    vc_hbm,
    mixed_ref,
    final_ref,
    qw,
    kvw,
    ow,
    gw,
    uw,
    dw,
    kc,
    vc,
    ag1,
    hid,
    hblock,
    xs,
    to_owner,
    at_owner,
    to_home,
    at_home,
    part1,
    peer1,
    out1,
    in1,
    mb,
    part2,
    peer2,
    sum2,
    out2,
    in2,
    load_sem,
    ag1_s,
    ag1_r,
    hid_s,
    hid_r,
    ag2_s,
    ag2_r,
    a1_s,
    a1_r,
    a2_s,
    a2_r,
    sw1_s,
    sw1_r,
    rs1_s,
    rs1_r,
    sw2_s,
    sw2_r,
    rs2_s,
    rs2_r,
):
    devices = pool * tensor
    rows, width = hidden_ref.shape
    requests = devices * rows
    half = tensor * rows
    block = width // tensor
    head_dim = query_gain_ref.shape[1]
    query_cols = qw.shape[1]
    key_cols = kvw.shape[0] // 2
    heads_here = query_cols // head_dim
    head_count = devices * heads_here
    kv_count = devices * key_cols // head_dim
    per_kv = devices // kv_count
    group = head_count // kv_count
    hidden_units = gw.shape[0]
    pieces = heads_here + 2
    span = 2 * SLOTS
    p = lax.axis_index("pool")
    t = lax.axis_index("tensor")
    me = p * tensor + t
    partner = {"pool": 1 - p, "tensor": t}

    barrier = pltpu.get_barrier_semaphore()

    def place(index):
        return {"pool": lax.div(index, tensor), "tensor": lax.rem(index, tensor)}

    for j in range(1, devices):
        pl.semaphore_signal(
            barrier, inc=1, device_id=place(lax.rem(me + j, devices)), device_id_type=MESH
        )

    loads = [
        pltpu.make_async_copy(a, b, load_sem.at[i])
        for i, (a, b) in enumerate(
            [
                (qw_hbm, qw),
                (kw_hbm, kvw.at[:key_cols]),
                (vw_hbm, kvw.at[key_cols:]),
                (kc_hbm, kc),
                (vc_hbm, vc),
                (ow_hbm, ow),
                (gw_hbm, gw),
                (uw_hbm, uw),
                (dw_hbm, dw),
            ]
        )
    ]
    for load in loads:
        load.start()

    def flip(j):
        out, bit = 0, 1
        while bit < tensor:
            digit = lax.rem(lax.div(t, bit), 2)
            out = out + bit * (1 - digit if (j // bit) % 2 else digit)
            bit *= 2
        return out

    near = [flip(j) for j in range(tensor)]
    around = range(1, tensor)

    def remote(source, target, sent, received, where):
        return pltpu.make_async_remote_copy(
            src_ref=source,
            dst_ref=target,
            send_sem=sent,
            recv_sem=received,
            device_id=where,
            device_id_type=MESH,
        )

    def in_plane(other):
        return {"pool": p, "tensor": other}

    class Gather:
        def __init__(self, buffer, sent, received):
            self.buffer, self.sent, self.received = buffer, sent, received

        def slot(self, q, index, k, where):
            at = self.buffer.at[q, index]
            return remote(at, at, self.sent.at[k], self.received.at[q, index], where)

        def send(self):
            for j in around:
                self.slot(p, t, j, in_plane(near[j])).start()
            self.slot(p, t, 0, partner).start()

        def forward(self, j):
            self.slot(p, near[j], tensor + j, partner).wait_recv()
            self.slot(p, near[j], tensor + j, partner).start()

        def across(self, j):
            self.slot(1 - p, near[j], 0, partner).wait_recv()

        def finish(self):
            self.slot(p, t, 0, partner).wait_send()
            for j in around:
                self.slot(p, t, j, in_plane(near[j])).wait_send()
                self.slot(p, near[j], tensor + j, partner).wait_send()

    first = Gather(ag1, ag1_s, ag1_r)
    second = Gather(mb, ag2_s, ag2_r)

    def hidden_copy(j, index):
        lanes = pl.ds(pl.multiple_of(near[j] * block, block), block)
        return remote(
            hidden_ref.at[:, lanes], hid.at[index], hid_s.at[j], hid_r.at[index], in_plane(near[j])
        )

    hidden = hidden_ref[...].astype(F32)
    ag1[p, t] = rms_scale(hidden, input_gain_ref[...]).astype(BF16)

    slot_row = slot_ref[...]
    length_row = length_ref[...]

    def iota(shape, dim):
        return lax.broadcasted_iota(jnp.int32, shape, dim)

    def hot(mask):
        return mask.astype(F32).astype(BF16)

    spread = hot(iota((requests, pieces * requests), 0) == lax.rem(iota((requests, pieces * requests), 1), requests))
    slot_wide = jnp.broadcast_to(slot_row, (span, requests))
    slot_tiled = jnp.dot(
        slot_wide.astype(F32).astype(BF16), spread, preferred_element_type=F32
    ).astype(jnp.int32)[:1]
    tall = devices * pieces * SLOTS
    row = iota((tall, pieces * requests), 0)
    col = iota((tall, pieces * requests), 1)
    wanted = lax.div(row, pieces * SLOTS) * SLOTS + lax.rem(row, SLOTS)
    scatter_hot = hot(
        (lax.rem(lax.div(row, SLOTS), pieces) == lax.div(col, requests)) & (wanted == slot_tiled)
    )
    eye = iota((requests, requests), 0) == iota((requests, requests), 1)
    slot_col = jnp.sum(
        jnp.where(eye, jnp.broadcast_to(slot_row, (requests, requests)), 0).astype(F32),
        axis=1,
        keepdims=True,
    ).astype(jnp.int32)
    home = devices * heads_here * SLOTS
    col = iota((requests, home), 1)
    held = lax.div(col, heads_here * SLOTS) * SLOTS + lax.rem(col, SLOTS)
    which = lax.rem(lax.div(col, SLOTS), heads_here)
    gather_hot = jnp.concatenate(
        [hot((which == i) & (held == slot_col)) for i in range(heads_here)], axis=0
    )
    place_id = lax.rem(iota((span, requests), 0), SLOTS)
    length_wide = jnp.broadcast_to(length_row, (span, requests)).astype(F32)
    base = me * SLOTS
    slot_length = jnp.sum(
        jnp.where(slot_wide == base + place_id, length_wide, 0.0), axis=1, keepdims=True
    )
    slot_offset = jnp.sum(
        jnp.where((slot_wide >= base) & (slot_wide < base + place_id), length_wide, 0.0),
        axis=1,
        keepdims=True,
    )
    angles = slot_length * frequency_ref[...]
    cosine = jnp.cos(angles)
    lane = iota((span, head_dim), 1)
    sine_part = jnp.where(lane < head_dim // 2, -jnp.sin(angles), jnp.sin(angles))
    pool_tokens = kc.shape[0]
    token = iota((span, pool_tokens), 1).astype(F32)
    inside = jnp.where((token >= slot_offset) & (token < slot_offset + slot_length), 1.0, 0.0)

    def turn(values, scale, copies):
        scaled = rms_scale(values, scale)
        return scaled * jnp.tile(cosine, (copies, 1)) + pltpu.roll(
            scaled, head_dim // 2, 1
        ) * jnp.tile(sine_part, (copies, 1))

    def turned(left, weight):
        return lax.dot_general(left, weight, (((1,), (1,)), ((), ())), preferred_element_type=F32)

    pl.semaphore_wait(barrier, devices - 1)
    first.send()
    for j in around:
        hidden_copy(j, t).start()
    hid[t] = hidden_ref[:, pl.ds(pl.multiple_of(t * block, block), block)]
    for load in loads[:3]:
        load.wait()
    for j in around:
        first.forward(j)
    for index in range(tensor):
        xs[p, index * rows : (index + 1) * rows, :] = ag1[p, index].astype(F32)
    for j in range(tensor):
        first.across(j)
    for index in range(tensor):
        xs[1 - p, index * rows : (index + 1) * rows, :] = ag1[1 - p, index].astype(F32)

    left = jnp.concatenate([xs[q] for q in range(pool)], axis=0).astype(BF16)
    query_part = jnp.dot(left, qw[...], preferred_element_type=F32).astype(BF16)
    kv_part = turned(left, kvw[...]).astype(BF16)

    wide = iota((2 * key_cols, 2 * head_dim), 1)
    tall = iota((2 * key_cols, 2 * head_dim), 0)
    shift = lax.rem(me, per_kv) * key_cols
    aim = jnp.where(tall < key_cols, tall + shift, tall - key_cols + head_dim + shift)
    kv_wide = jnp.dot(kv_part, hot(aim == wide), preferred_element_type=F32).astype(BF16)
    stacked = jnp.concatenate(
        [query_part[:, i * head_dim : (i + 1) * head_dim] for i in range(heads_here)]
        + [kv_wide[:, :head_dim], kv_wide[:, head_dim:]],
        axis=0,
    )
    slots = jnp.dot(scatter_hot, stacked, preferred_element_type=F32).astype(BF16)
    deep = pieces * SLOTS
    for index in range(devices):
        to_owner[index] = slots[index * deep : (index + 1) * deep]

    def exchange(outgoing, incoming, sent, received):
        def copy(j, index):
            peer = lax.rem(me + j, devices)
            slot = peer if index is None else index
            return remote(
                outgoing.at[peer], incoming.at[slot], sent.at[j], received.at[slot], place(peer)
            )

        for j in range(1, devices):
            copy(j, me).start()
        incoming[me] = outgoing[me]

        def arrive():
            for j in range(1, devices):
                copy(j, None).wait_recv()

        def finish():
            for j in range(1, devices):
                copy(j, me).wait_send()

        return arrive, finish

    arrive, sent_a1 = exchange(to_owner, at_owner, a1_s, a1_r)

    for j in around:
        hidden_copy(j, near[j]).wait_recv()
    for index in range(tensor):
        hblock[index * rows : (index + 1) * rows, :] = hid[index].astype(F32)
    for load in loads[3:5]:
        load.wait()
    arrive()

    scale_factor = 1.0 / math.sqrt(head_dim)
    copies = group * SLOTS // span
    allowed = jnp.tile(inside, (copies, 1)) > 0.5
    upper = iota((span, head_dim), 0) < SLOTS
    deep = heads_here * SLOTS
    for k in range(kv_count):
        blocks = [at_owner[k * per_kv + j].astype(F32) for j in range(per_kv)]
        query = jnp.concatenate([b[:deep] for b in blocks], axis=0)
        both = blocks[0][deep:]
        for b in blocks[1:]:
            both = both + b[deep:]
        turned_over = pltpu.roll(both, SLOTS, 0)
        key_new = turn(jnp.where(upper, both, turned_over), key_gain_ref[...], 1)
        own_value = jnp.tile(jnp.where(upper, turned_over, both), (copies, 1))
        own_key = jnp.tile(key_new.astype(BF16).astype(F32), (copies, 1))
        query = turn(query, query_gain_ref[...], copies).astype(BF16)
        lanes = slice(k * head_dim, (k + 1) * head_dim)
        scores = turned(query, kc[:, lanes]) * scale_factor
        own_score = jnp.sum(query.astype(F32) * own_key, axis=1, keepdims=True) * scale_factor
        scores = jnp.where(allowed, scores, -1e30)
        largest = jnp.maximum(jnp.max(scores, axis=1, keepdims=True), own_score)
        weights = jnp.exp(scores - largest)
        own_weight = jnp.exp(own_score - largest)
        denominator = jnp.sum(weights, axis=1, keepdims=True) + own_weight
        summed = jnp.dot(weights.astype(BF16), vc[:, lanes], preferred_element_type=F32)
        summed = summed + own_weight.astype(BF16).astype(F32) * own_value
        head_out = summed / denominator
        for j in range(per_kv):
            to_home[k * per_kv + j] = head_out[j * deep : (j + 1) * deep]

    arrive, sent_a2 = exchange(to_home, at_home, a2_s, a2_r)
    loads[5].wait()
    arrive()
    back = jnp.concatenate([at_home[index] for index in range(devices)], axis=0).astype(BF16)
    gathered = jnp.dot(gather_hot, back, preferred_element_type=F32).astype(BF16)
    head_rows = jnp.concatenate(
        [gathered[i * requests : (i + 1) * requests] for i in range(heads_here)], axis=1
    )

    pairs = tensor // 2
    wide = 2 * block

    def swap(part, peer, sent, received, c):
        return remote(part.at[c, 1 - p], peer.at[c], sent.at[c], received.at[c], partner)

    def products(left, weight, part, peer, sent, received, order):
        for c in range(pairs):
            at = pl.ds(pl.multiple_of(order[c] * wide, wide), wide)
            product = jnp.dot(left, weight[:, at], preferred_element_type=F32)
            for q in range(pool):
                part[c, q] = product[q * half : (q + 1) * half].astype(BF16)
            swap(part, peer, sent, received, c).start()

    turn_of = [lax.rem(lax.div(t, 2) + 1 + c, pairs) for c in range(pairs)]
    products(head_rows, ow, part1, peer1, sw1_s, sw1_r, turn_of)

    def block_copy(k, other, slot):
        return remote(out1.at[other], in1.at[slot], rs1_s.at[k], rs1_r.at[slot], in_plane(other))

    for c in range(pairs):
        swap(part1, peer1, sw1_s, sw1_r, c).wait_recv()
        total = (peer1[c].astype(F32) + part1[c, p].astype(F32)).astype(BF16)
        for i in range(2):
            out1[2 * turn_of[c] + i] = total[:, i * block : (i + 1) * block]
        if c + 1 < pairs:
            for i in range(2):
                block_copy(2 * c + i, 2 * turn_of[c] + i, t).start()
    block_copy(tensor - 2, near[1], t).start()
    total = hblock[...] + out1[t].astype(F32)
    for j in around:
        block_copy(0, near[j], near[j]).wait_recv()
        total = total + in1[near[j]].astype(F32)
    mb[p, t] = total.astype(BF16)
    second.send()

    def part_of(j):
        at = pl.ds(pl.multiple_of(near[j] * block, block), block)
        values = jnp.concatenate([mb[q, near[j]] for q in range(pool)], axis=0).astype(F32)
        squares = values * values
        some = squares[:, :128]
        for i in range(1, block // 128):
            some = some + squares[:, i * 128 : (i + 1) * 128]
        scaled = (values * post_gain_ref[:, at]).astype(BF16)
        return some, turned(scaled, gw[:, at]), turned(scaled, uw[:, at])

    loads[6].wait()
    loads[7].wait()
    lead = 2
    sent_up_to = 0
    acc = None
    for j in range(tensor):
        while sent_up_to < min(j + lead, tensor - 1) and j > 0 or sent_up_to < j:
            sent_up_to += 1
            second.forward(sent_up_to)
        second.across(j)
        new = part_of(j)
        acc = new if acc is None else tuple(a + b for a, b in zip(acc, new))
    square, gate_part, up_part = acc
    mean = jnp.sum(square, axis=1, keepdims=True) * (1.0 / width)
    scale = lax.rsqrt(mean + eps)
    gate_part = gate_part * scale
    up_part = up_part * scale
    activated = (gate_part / (1.0 + jnp.exp(-gate_part)) * up_part).astype(BF16)

    loads[8].wait()
    products(activated, dw, part2, peer2, sw2_s, sw2_r, list(range(pairs)))

    def row_copy(c, j, slot):
        lanes = slice(c * wide, (c + 1) * wide)
        return remote(
            out2.at[near[j], :, lanes],
            in2.at[slot, :, lanes],
            rs2_s.at[c, j],
            rs2_r.at[c, slot],
            in_plane(near[j]),
        )

    for c in range(pairs):
        lanes = slice(c * wide, (c + 1) * wide)
        swap(part2, peer2, sw2_s, sw2_r, c).wait_recv()
        sum2[:, lanes] = peer2[c].astype(F32) + part2[c, p].astype(F32)
        for index in range(tensor):
            out2[index, :, lanes] = sum2[index * rows : (index + 1) * rows, lanes].astype(BF16)
        for j in around:
            row_copy(c, j, t).start()

    pick = hot(iota((8, requests), 1) == me * rows + iota((8, requests), 0))
    mixed = jnp.concatenate(
        [
            jnp.dot(
                pick,
                jnp.concatenate([mb[q, index] for q in range(pool)], axis=0),
                preferred_element_type=F32,
            )[:rows]
            for index in range(tensor)
        ],
        axis=1,
    )
    mixed_ref[...] = mixed.astype(BF16)
    first.finish()
    sent_a1()
    sent_a2()
    second.finish()
    for j in around:
        hidden_copy(j, t).wait_send()
    for c in range(pairs):
        swap(part1, peer1, sw1_s, sw1_r, c).wait_send()
        swap(part2, peer2, sw2_s, sw2_r, c).wait_send()
    for c in range(pairs - 1):
        for i in range(2):
            block_copy(2 * c + i, 2 * turn_of[c] + i, t).wait_send()
    block_copy(tensor - 2, near[1], t).wait_send()

    for c in range(pairs):
        lanes = slice(c * wide, (c + 1) * wide)
        total = mixed[:, lanes]
        lowered = out2[t, :, lanes].astype(F32)
        for j in around:
            row_copy(c, j, near[j]).wait_recv()
            lowered = lowered + in2[near[j], :, lanes].astype(F32)
        final_ref[:, lanes] = (total + lowered).astype(BF16)
    for c in range(pairs):
        for j in around:
            row_copy(c, j, t).wait_send()


def fused(pool, tensor, *operands):
    (
        hidden,
        input_gain,
        query_weight,
        key_weight,
        value_weight,
        query_gain,
        key_gain,
        output_weight,
        post_gain,
        gate_weight,
        up_weight,
        down_weight,
        key_cache,
        value_cache,
        lengths,
        request_slot,
    ) = operands
    devices = pool * tensor
    rows, width = hidden.shape
    head_dim = query_gain.shape[0]
    query_cols = query_weight.shape[1]
    key_cols = key_weight.shape[1]
    heads_here = query_cols // head_dim
    half = tensor * rows
    block = width // tensor
    pairs = tensor // 2
    half_width = head_dim // 2
    frequency = theta ** (-np.arange(half_width) * 2.0 / head_dim)
    frequency = np.concatenate([frequency, frequency])[None, :].astype(np.float32)
    gate_turned, up_turned = gate_weight.T, up_weight.T
    dma = pltpu.SemaphoreType.DMA
    deep = (heads_here + 2) * SLOTS
    scratch = [
        pltpu.VMEM(query_weight.shape, BF16),
        pltpu.VMEM((2 * key_cols, width), BF16),
        pltpu.VMEM(output_weight.shape, BF16),
        pltpu.VMEM(gate_turned.shape, BF16),
        pltpu.VMEM(up_turned.shape, BF16),
        pltpu.VMEM(down_weight.shape, BF16),
        pltpu.VMEM(key_cache.shape, BF16),
        pltpu.VMEM(value_cache.shape, BF16),
        pltpu.VMEM((pool, tensor, rows, width), BF16),
        pltpu.VMEM((tensor, rows, block), BF16),
        pltpu.VMEM((half, block), F32),
        pltpu.VMEM((pool, half, width), F32),
        pltpu.VMEM((devices, deep, head_dim), BF16),
        pltpu.VMEM((devices, deep, head_dim), BF16),
        pltpu.VMEM((devices, heads_here * SLOTS, head_dim), F32),
        pltpu.VMEM((devices, heads_here * SLOTS, head_dim), F32),
        pltpu.VMEM((pairs, pool, half, 2 * block), BF16),
        pltpu.VMEM((pairs, half, 2 * block), BF16),
        pltpu.VMEM((tensor, half, block), BF16),
        pltpu.VMEM((tensor, half, block), BF16),
        pltpu.VMEM((pool, tensor, half, block), BF16),
        pltpu.VMEM((pairs, pool, half, 2 * block), BF16),
        pltpu.VMEM((pairs, half, 2 * block), BF16),
        pltpu.VMEM((half, width), F32),
        pltpu.VMEM((tensor, rows, width), BF16),
        pltpu.VMEM((tensor, rows, width), BF16),
        dma((9,)),
        dma((2 * tensor,)),
        dma((pool, tensor)),
        dma((tensor,)),
        dma((tensor,)),
        dma((2 * tensor,)),
        dma((pool, tensor)),
        dma((devices,)),
        dma((devices,)),
        dma((devices,)),
        dma((devices,)),
        dma((pairs,)),
        dma((pairs,)),
        dma((tensor,)),
        dma((tensor,)),
        dma((pairs,)),
        dma((pairs,)),
        dma((pairs, tensor)),
        dma((pairs, tensor)),
    ]
    vmem = pl.BlockSpec(memory_space=pltpu.VMEM)
    hbm = pl.BlockSpec(memory_space=pl.ANY)
    row = jax.ShapeDtypeStruct(hidden.shape, BF16)
    return pl.pallas_call(
        functools.partial(step_kernel, pool, tensor),
        out_shape=(row, row),
        in_specs=[vmem] * 8 + [hbm] * 9,
        out_specs=(vmem, vmem),
        scratch_shapes=scratch,
        compiler_params=pltpu.CompilerParams(
            collective_id=0, has_side_effects=True, vmem_limit_bytes=62 * 1024 * 1024
        ),
    )(
        hidden,
        input_gain[None, :],
        query_gain[None, :],
        key_gain[None, :],
        post_gain[None, :],
        lengths[None, :],
        request_slot[None, :],
        frequency,
        query_weight,
        key_weight.T,
        value_weight.T,
        output_weight,
        gate_turned,
        up_turned,
        down_weight,
        key_cache,
        value_cache,
    )


def dispatch(pool, tensor, *operands):
    rows, width = operands[0].shape
    query_cols = operands[2].shape[1]
    key_cols = operands[3].shape[1]
    head_dim = operands[5].shape[0]
    devices = pool * tensor
    lanes = width % (tensor * 128) == 0 and head_dim == 128
    paired = tensor >= 4 and tensor & (tensor - 1) == 0 and tensor * rows == 16
    heads = query_cols == 2 * head_dim and head_dim % key_cols == 0
    few = devices * SLOTS <= 256 and devices * rows * 4 % 128 == 0
    if pool == 2 and lanes and paired and heads and few:
        return fused(pool, tensor, *operands)
    return on_device(*operands)


def solution(mesh):
    placed = (
        P(("groups", "pool", "tensor"), None),
        P(),
        P(None, ("pool", "tensor")),
        P(None, ("pool", "tensor")),
        P(None, ("pool", "tensor")),
        P(),
        P(),
        P(("pool", "tensor"), None),
        P(),
        P(None, ("pool", "tensor")),
        P(None, ("pool", "tensor")),
        P(("pool", "tensor"), None),
        P(("groups", "pool", "tensor"), None),
        P(("groups", "pool", "tensor"), None),
        P("groups"),
        P("groups"),
    )
    return jax.shard_map(
        functools.partial(dispatch, mesh.shape["pool"], mesh.shape["tensor"]),
        mesh=mesh,
        in_specs=placed,
        out_specs=(P(("groups", "pool", "tensor"), None), P(("groups", "pool", "tensor"), None)),
        check_vma=False,
    )
```

```python
import functools
import math

import jax
import jax.numpy as jnp
import numpy as np
from jax import lax
from jax.experimental import pallas as pl
from jax.experimental.pallas import tpu as pltpu
from jax.sharding import PartitionSpec as P

SLOTS = 4


eps = 1e-06
theta = 1000000.0


def rms_scale(values, scales):
    values = values.astype(jnp.float32)
    return values * lax.rsqrt(jnp.mean(values * values, axis=-1, keepdims=True) + eps) * scales


def rotate(values, position):
    half_width = values.shape[-1] // 2
    frequency = theta ** (-jnp.arange(half_width, dtype=jnp.float32) * 2.0 / values.shape[-1])
    angles = position * frequency
    cosine = jnp.cos(angles)
    sine_part = jnp.sin(angles)
    front_half = values[..., :half_width]
    back_half = values[..., half_width:]
    return jnp.concatenate(
        [front_half * cosine - back_half * sine_part, back_half * cosine + front_half * sine_part],
        axis=-1,
    )


def on_device(
    hidden,
    input_gain,
    query_weight,
    key_weight,
    value_weight,
    query_gain,
    key_gain,
    output_weight,
    post_gain,
    gate_weight,
    up_weight,
    down_weight,
    key_cache,
    value_cache,
    lengths,
    request_slot,
):
    devices = lax.axis_size(("pool", "tensor"))
    device_index = lax.axis_index(("pool", "tensor"))
    local_rows = hidden.shape[0]
    query_cols = query_weight.shape[1]
    key_cols = key_weight.shape[1]
    width_sent = query_cols + 2 * key_cols
    head_dim = query_gain.shape[0]
    slot_count = SLOTS
    head_count = devices * query_cols // head_dim
    kv_count = devices * key_cols // head_dim
    group_size = head_count // kv_count
    normed = rms_scale(hidden, input_gain).astype(jnp.bfloat16)
    shard_rows = lax.all_gather(normed, ("pool", "tensor"), axis=0, tiled=True)
    query_part = jnp.dot(shard_rows, query_weight, preferred_element_type=jnp.float32)
    key_part = jnp.dot(shard_rows, key_weight, preferred_element_type=jnp.float32)
    value_part = jnp.dot(shard_rows, value_weight, preferred_element_type=jnp.float32)
    projected = jnp.concatenate([query_part, key_part, value_part], axis=1).astype(jnp.bfloat16)
    outgoing = (
        jnp.zeros((devices * slot_count, width_sent), jnp.bfloat16).at[request_slot].set(projected)
    )
    outgoing = outgoing.reshape(devices, slot_count, width_sent)
    arrived = lax.all_to_all(
        outgoing, ("pool", "tensor"), split_axis=0, concat_axis=2, tiled=True
    ).reshape(slot_count, devices, width_sent)
    query_full = arrived[:, :, :query_cols].reshape(slot_count, head_count, head_dim)
    key_full = arrived[:, :, query_cols : query_cols + key_cols].reshape(
        slot_count, kv_count, head_dim
    )
    value_new = arrived[:, :, query_cols + key_cols :].reshape(slot_count, kv_count, head_dim)
    slot_ids = device_index * slot_count + jnp.arange(slot_count, dtype=jnp.int32)
    matches = request_slot[None, :] == slot_ids[:, None]
    slot_length = jnp.sum(jnp.where(matches, lengths[None, :], 0), axis=1)
    owner_of = request_slot // slot_count
    within = request_slot % slot_count
    earlier = (owner_of[None, :] == device_index) & (
        within[None, :] < jnp.arange(slot_count, dtype=jnp.int32)[:, None]
    )
    slot_offset = jnp.sum(jnp.where(earlier, lengths[None, :], 0), axis=1)
    position = slot_length.astype(jnp.float32)[:, None, None]
    query_heads = rotate(rms_scale(query_full, query_gain), position).astype(jnp.bfloat16)
    query_heads = query_heads.reshape(slot_count, kv_count, group_size, head_dim)
    key_new = rotate(rms_scale(key_full, key_gain), position).astype(jnp.bfloat16)
    pool_tokens = key_cache.shape[0]
    cached_keys = key_cache.reshape(pool_tokens, kv_count, head_dim)
    cached_values = value_cache.reshape(pool_tokens, kv_count, head_dim)
    scale_factor = 1.0 / math.sqrt(head_dim)
    scores = (
        jnp.einsum("skgd,tkd->skgt", query_heads, cached_keys, preferred_element_type=jnp.float32)
        * scale_factor
    )
    own_score = (
        jnp.einsum("skgd,skd->skg", query_heads, key_new, preferred_element_type=jnp.float32)
        * scale_factor
    )
    token_pos = jnp.arange(pool_tokens, dtype=jnp.int32)
    inside = (token_pos[None, :] >= slot_offset[:, None]) & (
        token_pos[None, :] < (slot_offset + slot_length)[:, None]
    )
    inside = inside[:, None, None, :]
    largest = jnp.maximum(jnp.max(jnp.where(inside, scores, -1e30), axis=3), own_score)
    weights = jnp.where(inside, jnp.exp(scores - largest[..., None]), 0.0)
    own_weight = jnp.exp(own_score - largest)
    denominator = jnp.sum(weights, axis=3) + own_weight
    summed = jnp.einsum(
        "skgt,tkd->skgd",
        weights.astype(jnp.bfloat16),
        cached_values,
        preferred_element_type=jnp.float32,
    )
    own_low = own_weight.astype(jnp.bfloat16).astype(jnp.float32)
    summed = summed + own_low[..., None] * value_new.astype(jnp.float32)[:, :, None, :]
    head_out = (
        (summed / denominator[..., None])
        .astype(jnp.bfloat16)
        .reshape(slot_count, devices, query_cols)
    )
    returned = lax.all_to_all(head_out, ("pool", "tensor"), split_axis=1, concat_axis=0, tiled=True)
    head_rows = returned.reshape(devices * slot_count, query_cols)[request_slot]
    partial_value = jnp.dot(head_rows, output_weight, preferred_element_type=jnp.float32)
    row_start = device_index * local_rows
    own_part = lax.dynamic_slice_in_dim(partial_value, row_start, local_rows, 0) + hidden.astype(
        jnp.float32
    )
    partial_value = lax.dynamic_update_slice_in_dim(partial_value, own_part, row_start, 0)
    totals = lax.psum(partial_value, ("pool", "tensor"))
    mixed_all = totals.astype(jnp.bfloat16)
    mixed_rows = lax.dynamic_slice_in_dim(mixed_all, row_start, local_rows, 0)
    post_normed = rms_scale(mixed_all, post_gain).astype(jnp.bfloat16)
    gate_part = jnp.dot(post_normed, gate_weight, preferred_element_type=jnp.float32)
    up_part = jnp.dot(post_normed, up_weight, preferred_element_type=jnp.float32)
    activated = (jax.nn.silu(gate_part) * up_part).astype(jnp.bfloat16)
    lowered = lax.psum_scatter(
        jnp.dot(activated, down_weight, preferred_element_type=jnp.float32),
        ("pool", "tensor"),
        scatter_dimension=0,
        tiled=True,
    )
    final_rows = (mixed_rows.astype(jnp.float32) + lowered).astype(jnp.bfloat16)
    return (mixed_rows, final_rows)


MESH = pl.DeviceIdType.MESH
F32 = jnp.float32
BF16 = jnp.bfloat16
CUTS = 2


def step_kernel(
    pool,
    tensor,
    hidden_hbm,
    slot_hbm,
    length_hbm,
    input_gain_hbm,
    frequency_hbm,
    query_gain_hbm,
    key_gain_hbm,
    post_gain_hbm,
    qw_hbm,
    kw_hbm,
    vw_hbm,
    ow_hbm,
    gw_hbm,
    uw_hbm,
    dw_hbm,
    kc_hbm,
    vc_hbm,
    mixed_ref,
    added_ref,
    hidden_ref,
    slot_ref,
    length_ref,
    input_gain_ref,
    frequency_ref,
    query_gain_ref,
    key_gain_ref,
    post_gain_ref,
    qw,
    kvw,
    ow,
    gw,
    uw,
    dw,
    kc,
    vc,
    ag1,
    hid,
    hblock,
    xs,
    to_owner,
    at_owner,
    to_home,
    at_home,
    part1,
    peer1,
    out1,
    in1,
    mb,
    part2,
    peer2,
    sum2,
    out2,
    in2,
    small_sem,
    load_sem,
    ag1_s,
    ag1_r,
    hid_s,
    hid_r,
    ag2_s,
    ag2_r,
    a1_s,
    a1_r,
    a2_s,
    a2_r,
    sw1_s,
    sw1_r,
    rs1_s,
    rs1_r,
    sw2_s,
    sw2_r,
    rs2_s,
    rs2_r,
):
    devices = pool * tensor
    rows, width = hidden_ref.shape
    requests = devices * rows
    half = tensor * rows
    block = width // tensor
    head_dim = query_gain_ref.shape[1]
    query_cols = qw.shape[1]
    key_cols = kvw.shape[0] // 2
    heads_here = query_cols // head_dim
    head_count = devices * heads_here
    kv_count = devices * key_cols // head_dim
    per_kv = devices // kv_count
    group = head_count // kv_count
    hidden_units = gw.shape[0]
    pieces = heads_here + 2
    span = 2 * SLOTS
    p = lax.axis_index("pool")
    t = lax.axis_index("tensor")
    me = p * tensor + t
    partner = {"pool": 1 - p, "tensor": t}

    barrier = pltpu.get_barrier_semaphore()

    def place(index):
        return {"pool": lax.div(index, tensor), "tensor": lax.rem(index, tensor)}

    for j in range(1, devices):
        pl.semaphore_signal(
            barrier, inc=1, device_id=place(lax.rem(me + j, devices)), device_id_type=MESH
        )

    smalls = [
        pltpu.make_async_copy(a, b, small_sem.at[i])
        for i, (a, b) in enumerate(
            [
                (hidden_hbm, hidden_ref),
                (slot_hbm, slot_ref),
                (length_hbm, length_ref),
                (input_gain_hbm, input_gain_ref),
                (frequency_hbm, frequency_ref),
                (query_gain_hbm, query_gain_ref),
                (key_gain_hbm, key_gain_ref),
                (post_gain_hbm, post_gain_ref),
            ]
        )
    ]
    for load in smalls:
        load.start()

    loads = [
        pltpu.make_async_copy(a, b, load_sem.at[i])
        for i, (a, b) in enumerate(
            [
                (qw_hbm, qw),
                (kw_hbm, kvw.at[:key_cols]),
                (vw_hbm, kvw.at[key_cols:]),
                (kc_hbm, kc),
                (vc_hbm, vc),
                (ow_hbm, ow),
                (gw_hbm, gw),
                (uw_hbm, uw),
                (dw_hbm, dw),
            ]
        )
    ]

    def flip(j):
        out, bit = 0, 1
        while bit < tensor:
            digit = lax.rem(lax.div(t, bit), 2)
            out = out + bit * (1 - digit if (j // bit) % 2 else digit)
            bit *= 2
        return out

    around = range(1, tensor)
    spin = [lax.rem(t + j, tensor) for j in range(tensor)]
    if tensor == 8:
        deep, side = lax.div(t, 2), lax.rem(t, 2)
        upper = lax.div(deep, 2)
        layers = [deep, deep + 1 - 2 * lax.rem(deep, 2), 2 - upper, 3 - 3 * upper]
        near = [2 * layer + q for layer in layers for q in (side, 1 - side)]
    else:
        near = [flip(j) for j in range(tensor)]

    def remote(source, target, sent, received, where):
        return pltpu.make_async_remote_copy(
            src_ref=source,
            dst_ref=target,
            send_sem=sent,
            recv_sem=received,
            device_id=where,
            device_id_type=MESH,
        )

    def in_plane(other):
        return {"pool": p, "tensor": other}

    class Gather:
        def __init__(self, buffer, sent, received):
            self.buffer, self.sent, self.received = buffer, sent, received

        def slot(self, q, index, k, where):
            at = self.buffer.at[q, index]
            return remote(at, at, self.sent.at[k], self.received.at[q, index], where)

        def send(self):
            for j in around:
                self.slot(p, t, j, in_plane(spin[j])).start()
            self.slot(p, t, 0, partner).start()

        def forward(self, j):
            self.slot(p, near[j], tensor + j, partner).wait_recv()
            self.slot(p, near[j], tensor + j, partner).start()

        def across(self, j):
            self.slot(1 - p, near[j], 0, partner).wait_recv()

        def finish(self):
            self.slot(p, t, 0, partner).wait_send()
            for j in around:
                self.slot(p, t, j, in_plane(spin[j])).wait_send()
                self.slot(p, near[j], tensor + j, partner).wait_send()

    first = Gather(ag1, ag1_s, ag1_r)
    second = Gather(mb, ag2_s, ag2_r)

    def hidden_copy(j, index):
        lanes = pl.ds(pl.multiple_of(near[j] * block, block), block)
        return remote(
            hidden_ref.at[:, lanes], hid.at[index], hid_s.at[j], hid_r.at[index], in_plane(near[j])
        )

    for load in smalls:
        load.wait()
    for load in loads:
        load.start()
    hidden = hidden_ref[...].astype(F32)
    ag1[p, t] = rms_scale(hidden, input_gain_ref[...]).astype(BF16)

    slot_row = slot_ref[...]
    length_row = length_ref[...]

    def iota(shape, dim):
        return lax.broadcasted_iota(jnp.int32, shape, dim)

    def hot(mask):
        return mask.astype(F32).astype(BF16)

    spread = hot(iota((requests, pieces * requests), 0) == lax.rem(iota((requests, pieces * requests), 1), requests))
    slot_wide = jnp.broadcast_to(slot_row, (span, requests))
    slot_tiled = jnp.dot(
        slot_wide.astype(F32).astype(BF16), spread, preferred_element_type=F32
    ).astype(jnp.int32)[:1]
    tall = devices * pieces * SLOTS
    row = iota((tall, pieces * requests), 0)
    col = iota((tall, pieces * requests), 1)
    wanted = lax.div(row, pieces * SLOTS) * SLOTS + lax.rem(row, SLOTS)
    scatter_hot = hot(
        (lax.rem(lax.div(row, SLOTS), pieces) == lax.div(col, requests)) & (wanted == slot_tiled)
    )
    eye = iota((requests, requests), 0) == iota((requests, requests), 1)
    slot_col = jnp.sum(
        jnp.where(eye, jnp.broadcast_to(slot_row, (requests, requests)), 0).astype(F32),
        axis=1,
        keepdims=True,
    ).astype(jnp.int32)
    home = devices * heads_here * SLOTS
    col = iota((requests, home), 1)
    held = lax.div(col, heads_here * SLOTS) * SLOTS + lax.rem(col, SLOTS)
    which = lax.rem(lax.div(col, SLOTS), heads_here)
    gather_hot = jnp.concatenate(
        [hot((which == i) & (held == slot_col)) for i in range(heads_here)], axis=0
    )
    place_id = lax.rem(iota((span, requests), 0), SLOTS)
    length_wide = jnp.broadcast_to(length_row, (span, requests)).astype(F32)
    base = me * SLOTS
    slot_length = jnp.sum(
        jnp.where(slot_wide == base + place_id, length_wide, 0.0), axis=1, keepdims=True
    )
    slot_offset = jnp.sum(
        jnp.where((slot_wide >= base) & (slot_wide < base + place_id), length_wide, 0.0),
        axis=1,
        keepdims=True,
    )
    angles = slot_length * frequency_ref[...]
    cosine = jnp.cos(angles)
    lane = iota((span, head_dim), 1)
    sine_part = jnp.where(lane < head_dim // 2, -jnp.sin(angles), jnp.sin(angles))
    pool_tokens = kc.shape[0]
    token = iota((span, pool_tokens), 1).astype(F32)
    inside = jnp.where((token >= slot_offset) & (token < slot_offset + slot_length), 1.0, 0.0)

    def turn(values, scale, copies):
        scaled = rms_scale(values, scale)
        return scaled * jnp.tile(cosine, (copies, 1)) + pltpu.roll(
            scaled, head_dim // 2, 1
        ) * jnp.tile(sine_part, (copies, 1))

    def turned(left, weight):
        return lax.dot_general(left, weight, (((1,), (1,)), ((), ())), preferred_element_type=F32)

    pl.semaphore_wait(barrier, devices - 1)
    first.send()
    for j in around:
        hidden_copy(j, t).start()
    hid[t] = hidden_ref[:, pl.ds(pl.multiple_of(t * block, block), block)]
    for load in loads[:3]:
        load.wait()
    for j in around:
        first.forward(j)
    for index in range(tensor):
        xs[p, index * rows : (index + 1) * rows, :] = ag1[p, index].astype(F32)
    for j in range(tensor):
        first.across(j)
    for index in range(tensor):
        xs[1 - p, index * rows : (index + 1) * rows, :] = ag1[1 - p, index].astype(F32)

    left = jnp.concatenate([xs[q] for q in range(pool)], axis=0).astype(BF16)
    query_part = jnp.dot(left, qw[...], preferred_element_type=F32).astype(BF16)
    kv_part = turned(left, kvw[...]).astype(BF16)

    wide = iota((2 * key_cols, 2 * head_dim), 1)
    tall = iota((2 * key_cols, 2 * head_dim), 0)
    shift = lax.rem(me, per_kv) * key_cols
    aim = jnp.where(tall < key_cols, tall + shift, tall - key_cols + head_dim + shift)
    kv_wide = jnp.dot(kv_part, hot(aim == wide), preferred_element_type=F32).astype(BF16)
    stacked = jnp.concatenate(
        [query_part[:, i * head_dim : (i + 1) * head_dim] for i in range(heads_here)]
        + [kv_wide[:, :head_dim], kv_wide[:, head_dim:]],
        axis=0,
    )
    slots = jnp.dot(scatter_hot, stacked, preferred_element_type=F32).astype(BF16)
    deep = pieces * SLOTS
    for index in range(devices):
        to_owner[index] = slots[index * deep : (index + 1) * deep]

    own_group, own_seat = lax.div(me, per_kv), lax.rem(me, per_kv)
    side_groups = kv_count // pool
    depth = lax.rem(own_group, side_groups)
    turns = [(0, 0)] + [(q, h) for q in (0, 1) for h in range(1, side_groups)] + [(1, 0)]
    groups = [
        (p if q == 0 else 1 - p) * side_groups + lax.rem(depth + h, side_groups) for q, h in turns
    ]

    def members(g):
        if g == 0:
            return [(j, groups[0] * per_kv + lax.rem(own_seat + j, per_kv)) for j in range(1, per_kv)]
        return [(g * per_kv + j, groups[g] * per_kv + j) for j in range(per_kv)]

    everyone = [member for g in range(kv_count) for member in members(g)]

    def post(outgoing, incoming, sent, received, number, peer):
        return remote(
            outgoing.at[peer], incoming.at[me], sent.at[number], received.at[me], place(peer)
        )

    def arrival(outgoing, incoming, sent, received, number, peer):
        return remote(
            outgoing.at[peer], incoming.at[peer], sent.at[number], received.at[peer], place(peer)
        )

    one = (to_owner, at_owner, a1_s, a1_r)
    two = (to_home, at_home, a2_s, a2_r)
    for member in everyone[::-1]:
        post(*one, *member).start()
    at_owner[me] = to_owner[me]

    for j in around:
        hidden_copy(j, near[j]).wait_recv()
    for index in range(tensor):
        hblock[index * rows : (index + 1) * rows, :] = hid[index].astype(F32)
    for load in loads[3:5]:
        load.wait()

    scale_factor = 1.0 / math.sqrt(head_dim)
    copies = group * SLOTS // span
    allowed = jnp.tile(inside, (copies, 1)) > 0.5
    upper = iota((span, head_dim), 0) < SLOTS
    deep = heads_here * SLOTS
    for g in range(kv_count):
        for member in members(g):
            arrival(*one, *member).wait_recv()
        k = groups[g]
        blocks = [at_owner[k * per_kv + j].astype(F32) for j in range(per_kv)]
        query = jnp.concatenate([b[:deep] for b in blocks], axis=0)
        both = blocks[0][deep:]
        for b in blocks[1:]:
            both = both + b[deep:]
        turned_over = pltpu.roll(both, SLOTS, 0)
        key_new = turn(jnp.where(upper, both, turned_over), key_gain_ref[...], 1)
        own_value = jnp.tile(jnp.where(upper, turned_over, both), (copies, 1))
        own_key = jnp.tile(key_new.astype(BF16).astype(F32), (copies, 1))
        query = turn(query, query_gain_ref[...], copies).astype(BF16)
        lanes = pl.ds(pl.multiple_of(k * head_dim, head_dim), head_dim)
        scores = turned(query, kc[:, lanes]) * scale_factor
        own_score = jnp.sum(query.astype(F32) * own_key, axis=1, keepdims=True) * scale_factor
        scores = jnp.where(allowed, scores, -1e30)
        largest = jnp.maximum(jnp.max(scores, axis=1, keepdims=True), own_score)
        weights = jnp.exp(scores - largest)
        own_weight = jnp.exp(own_score - largest)
        denominator = jnp.sum(weights, axis=1, keepdims=True) + own_weight
        summed = jnp.dot(weights.astype(BF16), vc[:, lanes], preferred_element_type=F32)
        summed = summed + own_weight.astype(BF16).astype(F32) * own_value
        head_out = summed / denominator
        for j in range(per_kv):
            to_home[k * per_kv + j] = head_out[j * deep : (j + 1) * deep]
        for member in members(g):
            post(*two, *member).start()
    at_home[me] = to_home[me]

    loads[5].wait()
    for member in everyone:
        arrival(*two, *member).wait_recv()
    back = jnp.concatenate([at_home[index] for index in range(devices)], axis=0).astype(BF16)
    gathered = jnp.dot(gather_hot, back, preferred_element_type=F32).astype(BF16)
    head_rows = jnp.concatenate(
        [gathered[i * requests : (i + 1) * requests] for i in range(heads_here)], axis=1
    )

    pairs = tensor // 2
    wide = 2 * block

    def swap(part, peer, sent, received, c):
        return remote(part.at[c, 1 - p], peer.at[c], sent.at[c], received.at[c], partner)

    def products(left, weight, part, peer, sent, received, order):
        wide = part.shape[-1]
        for c in range(part.shape[0]):
            at = pl.ds(pl.multiple_of(order[c] * wide, wide), wide)
            product = jnp.dot(left, weight[:, at], preferred_element_type=F32)
            for q in range(pool):
                part[c, q] = product[q * half : (q + 1) * half].astype(BF16)
            swap(part, peer, sent, received, c).start()

    turn_of = [lax.rem(lax.div(t, 2) + 1 + c, pairs) for c in range(pairs)]
    products(head_rows, ow, part1, peer1, sw1_s, sw1_r, turn_of)

    def block_copy(k, other, slot):
        return remote(out1.at[other], in1.at[slot], rs1_s.at[k], rs1_r.at[slot], in_plane(other))

    for c in range(pairs):
        swap(part1, peer1, sw1_s, sw1_r, c).wait_recv()
        total = (peer1[c].astype(F32) + part1[c, p].astype(F32)).astype(BF16)
        for i in range(2):
            out1[2 * turn_of[c] + i] = total[:, i * block : (i + 1) * block]
        if c + 1 < pairs:
            for i in range(2):
                block_copy(2 * c + i, 2 * turn_of[c] + i, t).start()
    block_copy(tensor - 2, near[1], t).start()
    total = hblock[...] + out1[t].astype(F32)
    for j in around:
        block_copy(0, near[j], near[j]).wait_recv()
        total = total + in1[near[j]].astype(F32)
    mb[p, t] = total.astype(BF16)
    second.send()

    def part_of(j):
        at = pl.ds(pl.multiple_of(near[j] * block, block), block)
        values = jnp.concatenate([mb[q, near[j]] for q in range(pool)], axis=0).astype(F32)
        squares = values * values
        some = squares[:, :128]
        for i in range(1, block // 128):
            some = some + squares[:, i * 128 : (i + 1) * 128]
        scaled = (values * post_gain_ref[:, at]).astype(BF16)
        return some, turned(scaled, gw[:, at]), turned(scaled, uw[:, at])

    loads[6].wait()
    loads[7].wait()
    lead = 2
    sent_up_to = 0
    acc = None
    for j in range(tensor):
        while sent_up_to < min(j + lead, tensor - 1) and j > 0 or sent_up_to < j:
            sent_up_to += 1
            second.forward(sent_up_to)
        second.across(j)
        new = part_of(j)
        acc = new if acc is None else tuple(a + b for a, b in zip(acc, new))
    square, gate_part, up_part = acc
    mean = jnp.sum(square, axis=1, keepdims=True) * (1.0 / width)
    scale = lax.rsqrt(mean + eps)
    gate_part = gate_part * scale
    up_part = up_part * scale
    activated = (gate_part / (1.0 + jnp.exp(-gate_part)) * up_part).astype(BF16)

    loads[8].wait()
    cuts = part2.shape[0]
    wide = width // cuts
    products(activated, dw, part2, peer2, sw2_s, sw2_r, list(range(cuts)))

    def row_copy(c, j, slot):
        lanes = slice(c * wide, (c + 1) * wide)
        return remote(
            out2.at[spin[j], :, lanes],
            in2.at[slot, :, lanes],
            rs2_s.at[c, j],
            rs2_r.at[c, slot],
            in_plane(spin[j]),
        )

    for c in range(cuts):
        lanes = slice(c * wide, (c + 1) * wide)
        swap(part2, peer2, sw2_s, sw2_r, c).wait_recv()
        sum2[:, lanes] = peer2[c].astype(F32) + part2[c, p].astype(F32)
        for index in range(tensor):
            out2[index, :, lanes] = sum2[index * rows : (index + 1) * rows, lanes].astype(BF16)
        for j in around:
            row_copy(c, j, t).start()

    pick = hot(iota((8, requests), 1) == me * rows + iota((8, requests), 0))
    mixed_ref[...] = jnp.concatenate(
        [
            jnp.dot(
                pick,
                jnp.concatenate([mb[q, index] for q in range(pool)], axis=0),
                preferred_element_type=F32,
            )[:rows]
            for index in range(tensor)
        ],
        axis=1,
    )
    first.finish()
    for member in everyone:
        post(*one, *member).wait_send()
        post(*two, *member).wait_send()
    second.finish()
    for j in around:
        hidden_copy(j, t).wait_send()
    for c in range(pairs):
        swap(part1, peer1, sw1_s, sw1_r, c).wait_send()
    for c in range(cuts):
        swap(part2, peer2, sw2_s, sw2_r, c).wait_send()
    for c in range(pairs - 1):
        for i in range(2):
            block_copy(2 * c + i, 2 * turn_of[c] + i, t).wait_send()
    block_copy(tensor - 2, near[1], t).wait_send()

    for c in range(cuts):
        lanes = slice(c * wide, (c + 1) * wide)
        total = out2[t, :, lanes].astype(F32)
        for j in around:
            row_copy(c, j, spin[j]).wait_recv()
            total = total + in2[spin[j], :, lanes].astype(F32)
        added_ref[:, lanes] = total
    for c in range(cuts):
        for j in around:
            row_copy(c, j, t).wait_send()


def fused(pool, tensor, *operands):
    (
        hidden,
        input_gain,
        query_weight,
        key_weight,
        value_weight,
        query_gain,
        key_gain,
        output_weight,
        post_gain,
        gate_weight,
        up_weight,
        down_weight,
        key_cache,
        value_cache,
        lengths,
        request_slot,
    ) = operands
    devices = pool * tensor
    rows, width = hidden.shape
    head_dim = query_gain.shape[0]
    query_cols = query_weight.shape[1]
    key_cols = key_weight.shape[1]
    heads_here = query_cols // head_dim
    half = tensor * rows
    block = width // tensor
    pairs = tensor // 2
    half_width = head_dim // 2
    frequency = theta ** (-np.arange(half_width) * 2.0 / head_dim)
    frequency = np.concatenate([frequency, frequency])[None, :].astype(np.float32)
    gate_turned, up_turned = gate_weight.T, up_weight.T
    dma = pltpu.SemaphoreType.DMA
    deep = (heads_here + 2) * SLOTS
    small = (
        hidden,
        request_slot[None, :],
        lengths[None, :],
        input_gain[None, :],
        frequency,
        query_gain[None, :],
        key_gain[None, :],
        post_gain[None, :],
    )
    scratch = [pltpu.VMEM(v.shape, v.dtype) for v in small] + [
        pltpu.VMEM(query_weight.shape, BF16),
        pltpu.VMEM((2 * key_cols, width), BF16),
        pltpu.VMEM(output_weight.shape, BF16),
        pltpu.VMEM(gate_turned.shape, BF16),
        pltpu.VMEM(up_turned.shape, BF16),
        pltpu.VMEM(down_weight.shape, BF16),
        pltpu.VMEM(key_cache.shape, BF16),
        pltpu.VMEM(value_cache.shape, BF16),
        pltpu.VMEM((pool, tensor, rows, width), BF16),
        pltpu.VMEM((tensor, rows, block), BF16),
        pltpu.VMEM((half, block), F32),
        pltpu.VMEM((pool, half, width), F32),
        pltpu.VMEM((devices, deep, head_dim), BF16),
        pltpu.VMEM((devices, deep, head_dim), BF16),
        pltpu.VMEM((devices, heads_here * SLOTS, head_dim), F32),
        pltpu.VMEM((devices, heads_here * SLOTS, head_dim), F32),
        pltpu.VMEM((pairs, pool, half, 2 * block), BF16),
        pltpu.VMEM((pairs, half, 2 * block), BF16),
        pltpu.VMEM((tensor, half, block), BF16),
        pltpu.VMEM((tensor, half, block), BF16),
        pltpu.VMEM((pool, tensor, half, block), BF16),
        pltpu.VMEM((CUTS, pool, half, width // CUTS), BF16),
        pltpu.VMEM((CUTS, half, width // CUTS), BF16),
        pltpu.VMEM((half, width), F32),
        pltpu.VMEM((tensor, rows, width), BF16),
        pltpu.VMEM((tensor, rows, width), BF16),
        dma((len(small),)),
        dma((9,)),
        dma((2 * tensor,)),
        dma((pool, tensor)),
        dma((tensor,)),
        dma((tensor,)),
        dma((2 * tensor,)),
        dma((pool, tensor)),
        dma((devices,)),
        dma((devices,)),
        dma((devices,)),
        dma((devices,)),
        dma((pairs,)),
        dma((pairs,)),
        dma((tensor,)),
        dma((tensor,)),
        dma((CUTS,)),
        dma((CUTS,)),
        dma((CUTS, tensor)),
        dma((CUTS, tensor)),
    ]
    vmem = pl.BlockSpec(memory_space=pltpu.VMEM)
    hbm = pl.BlockSpec(memory_space=pl.ANY)
    row = pltpu.VMEM(hidden.shape, F32)
    mixed, added = pl.pallas_call(
        functools.partial(step_kernel, pool, tensor),
        out_shape=(row, row),
        in_specs=[hbm] * (len(small) + 9),
        out_specs=(vmem, vmem),
        scratch_shapes=scratch,
        compiler_params=pltpu.CompilerParams(
            collective_id=0, has_side_effects=True, vmem_limit_bytes=62 * 1024 * 1024
        ),
    )(
        *small,
        query_weight,
        key_weight.T,
        value_weight.T,
        output_weight,
        gate_turned,
        up_turned,
        down_weight,
        key_cache,
        value_cache,
    )
    return mixed.astype(hidden.dtype), (mixed + added).astype(hidden.dtype)


def dispatch(pool, tensor, *operands):
    rows, width = operands[0].shape
    query_cols = operands[2].shape[1]
    key_cols = operands[3].shape[1]
    head_dim = operands[5].shape[0]
    devices = pool * tensor
    lanes = width % (tensor * 128) == 0 and head_dim == 128
    paired = tensor >= 4 and tensor & (tensor - 1) == 0 and tensor * rows == 16
    heads = query_cols == 2 * head_dim and head_dim % key_cols == 0
    few = devices * SLOTS <= 256 and devices * rows * 4 % 128 == 0
    if pool == 2 and lanes and paired and heads and few:
        return fused(pool, tensor, *operands)
    return on_device(*operands)


def solution(mesh):
    placed = (
        P(("groups", "pool", "tensor"), None),
        P(),
        P(None, ("pool", "tensor")),
        P(None, ("pool", "tensor")),
        P(None, ("pool", "tensor")),
        P(),
        P(),
        P(("pool", "tensor"), None),
        P(),
        P(None, ("pool", "tensor")),
        P(None, ("pool", "tensor")),
        P(("pool", "tensor"), None),
        P(("groups", "pool", "tensor"), None),
        P(("groups", "pool", "tensor"), None),
        P("groups"),
        P("groups"),
    )
    return jax.shard_map(
        functools.partial(dispatch, mesh.shape["pool"], mesh.shape["tensor"]),
        mesh=mesh,
        in_specs=placed,
        out_specs=(P(("groups", "pool", "tensor"), None), P(("groups", "pool", "tensor"), None)),
        check_vma=False,
    )
```

```python
import functools
import math

import jax
import jax.numpy as jnp
import numpy as np
from jax import lax
from jax.experimental import pallas as pl
from jax.experimental.pallas import tpu as pltpu
from jax.sharding import PartitionSpec as P

SLOTS = 4


eps = 1e-06
theta = 1000000.0


def rms_scale(values, scales):
    values = values.astype(jnp.float32)
    return values * lax.rsqrt(jnp.mean(values * values, axis=-1, keepdims=True) + eps) * scales


def rotate(values, position):
    half_width = values.shape[-1] // 2
    frequency = theta ** (-jnp.arange(half_width, dtype=jnp.float32) * 2.0 / values.shape[-1])
    angles = position * frequency
    cosine = jnp.cos(angles)
    sine_part = jnp.sin(angles)
    front_half = values[..., :half_width]
    back_half = values[..., half_width:]
    return jnp.concatenate(
        [front_half * cosine - back_half * sine_part, back_half * cosine + front_half * sine_part],
        axis=-1,
    )


def on_device(
    hidden,
    input_gain,
    query_weight,
    key_weight,
    value_weight,
    query_gain,
    key_gain,
    output_weight,
    post_gain,
    gate_weight,
    up_weight,
    down_weight,
    key_cache,
    value_cache,
    lengths,
    request_slot,
):
    devices = lax.axis_size(("pool", "tensor"))
    device_index = lax.axis_index(("pool", "tensor"))
    local_rows = hidden.shape[0]
    query_cols = query_weight.shape[1]
    key_cols = key_weight.shape[1]
    width_sent = query_cols + 2 * key_cols
    head_dim = query_gain.shape[0]
    slot_count = SLOTS
    head_count = devices * query_cols // head_dim
    kv_count = devices * key_cols // head_dim
    group_size = head_count // kv_count
    normed = rms_scale(hidden, input_gain).astype(jnp.bfloat16)
    shard_rows = lax.all_gather(normed, ("pool", "tensor"), axis=0, tiled=True)
    query_part = jnp.dot(shard_rows, query_weight, preferred_element_type=jnp.float32)
    key_part = jnp.dot(shard_rows, key_weight, preferred_element_type=jnp.float32)
    value_part = jnp.dot(shard_rows, value_weight, preferred_element_type=jnp.float32)
    projected = jnp.concatenate([query_part, key_part, value_part], axis=1).astype(jnp.bfloat16)
    outgoing = (
        jnp.zeros((devices * slot_count, width_sent), jnp.bfloat16).at[request_slot].set(projected)
    )
    outgoing = outgoing.reshape(devices, slot_count, width_sent)
    arrived = lax.all_to_all(
        outgoing, ("pool", "tensor"), split_axis=0, concat_axis=2, tiled=True
    ).reshape(slot_count, devices, width_sent)
    query_full = arrived[:, :, :query_cols].reshape(slot_count, head_count, head_dim)
    key_full = arrived[:, :, query_cols : query_cols + key_cols].reshape(
        slot_count, kv_count, head_dim
    )
    value_new = arrived[:, :, query_cols + key_cols :].reshape(slot_count, kv_count, head_dim)
    slot_ids = device_index * slot_count + jnp.arange(slot_count, dtype=jnp.int32)
    matches = request_slot[None, :] == slot_ids[:, None]
    slot_length = jnp.sum(jnp.where(matches, lengths[None, :], 0), axis=1)
    owner_of = request_slot // slot_count
    within = request_slot % slot_count
    earlier = (owner_of[None, :] == device_index) & (
        within[None, :] < jnp.arange(slot_count, dtype=jnp.int32)[:, None]
    )
    slot_offset = jnp.sum(jnp.where(earlier, lengths[None, :], 0), axis=1)
    position = slot_length.astype(jnp.float32)[:, None, None]
    query_heads = rotate(rms_scale(query_full, query_gain), position).astype(jnp.bfloat16)
    query_heads = query_heads.reshape(slot_count, kv_count, group_size, head_dim)
    key_new = rotate(rms_scale(key_full, key_gain), position).astype(jnp.bfloat16)
    pool_tokens = key_cache.shape[0]
    cached_keys = key_cache.reshape(pool_tokens, kv_count, head_dim)
    cached_values = value_cache.reshape(pool_tokens, kv_count, head_dim)
    scale_factor = 1.0 / math.sqrt(head_dim)
    scores = (
        jnp.einsum("skgd,tkd->skgt", query_heads, cached_keys, preferred_element_type=jnp.float32)
        * scale_factor
    )
    own_score = (
        jnp.einsum("skgd,skd->skg", query_heads, key_new, preferred_element_type=jnp.float32)
        * scale_factor
    )
    token_pos = jnp.arange(pool_tokens, dtype=jnp.int32)
    inside = (token_pos[None, :] >= slot_offset[:, None]) & (
        token_pos[None, :] < (slot_offset + slot_length)[:, None]
    )
    inside = inside[:, None, None, :]
    largest = jnp.maximum(jnp.max(jnp.where(inside, scores, -1e30), axis=3), own_score)
    weights = jnp.where(inside, jnp.exp(scores - largest[..., None]), 0.0)
    own_weight = jnp.exp(own_score - largest)
    denominator = jnp.sum(weights, axis=3) + own_weight
    summed = jnp.einsum(
        "skgt,tkd->skgd",
        weights.astype(jnp.bfloat16),
        cached_values,
        preferred_element_type=jnp.float32,
    )
    own_low = own_weight.astype(jnp.bfloat16).astype(jnp.float32)
    summed = summed + own_low[..., None] * value_new.astype(jnp.float32)[:, :, None, :]
    head_out = (
        (summed / denominator[..., None])
        .astype(jnp.bfloat16)
        .reshape(slot_count, devices, query_cols)
    )
    returned = lax.all_to_all(head_out, ("pool", "tensor"), split_axis=1, concat_axis=0, tiled=True)
    head_rows = returned.reshape(devices * slot_count, query_cols)[request_slot]
    partial_value = jnp.dot(head_rows, output_weight, preferred_element_type=jnp.float32)
    row_start = device_index * local_rows
    own_part = lax.dynamic_slice_in_dim(partial_value, row_start, local_rows, 0) + hidden.astype(
        jnp.float32
    )
    partial_value = lax.dynamic_update_slice_in_dim(partial_value, own_part, row_start, 0)
    totals = lax.psum(partial_value, ("pool", "tensor"))
    mixed_all = totals.astype(jnp.bfloat16)
    mixed_rows = lax.dynamic_slice_in_dim(mixed_all, row_start, local_rows, 0)
    post_normed = rms_scale(mixed_all, post_gain).astype(jnp.bfloat16)
    gate_part = jnp.dot(post_normed, gate_weight, preferred_element_type=jnp.float32)
    up_part = jnp.dot(post_normed, up_weight, preferred_element_type=jnp.float32)
    activated = (jax.nn.silu(gate_part) * up_part).astype(jnp.bfloat16)
    lowered = lax.psum_scatter(
        jnp.dot(activated, down_weight, preferred_element_type=jnp.float32),
        ("pool", "tensor"),
        scatter_dimension=0,
        tiled=True,
    )
    final_rows = (mixed_rows.astype(jnp.float32) + lowered).astype(jnp.bfloat16)
    return (mixed_rows, final_rows)


MESH = pl.DeviceIdType.MESH
F32 = jnp.float32
BF16 = jnp.bfloat16
CUTS = 2


def step_kernel(
    pool,
    tensor,
    hidden_hbm,
    slot_hbm,
    length_hbm,
    input_gain_hbm,
    frequency_hbm,
    query_gain_hbm,
    key_gain_hbm,
    post_gain_hbm,
    qw_hbm,
    kw_hbm,
    vw_hbm,
    ow_hbm,
    gw_hbm,
    uw_hbm,
    dw_hbm,
    kc_hbm,
    vc_hbm,
    mixed_ref,
    added_ref,
    hidden_ref,
    slot_ref,
    length_ref,
    input_gain_ref,
    frequency_ref,
    query_gain_ref,
    key_gain_ref,
    post_gain_ref,
    qw,
    kvw,
    ow,
    gw,
    uw,
    dw,
    kc,
    vc,
    ag1,
    hid,
    hblock,
    xs,
    to_owner,
    at_owner,
    to_home,
    at_home,
    part1,
    peer1,
    out1,
    in1,
    mb,
    part2,
    peer2,
    sum2,
    out2,
    in2,
    small_sem,
    load_sem,
    ag1_s,
    ag1_r,
    hid_s,
    hid_r,
    ag2_s,
    ag2_r,
    a1_s,
    a1_r,
    a2_s,
    a2_r,
    sw1_s,
    sw1_r,
    rs1_s,
    rs1_r,
    sw2_s,
    sw2_r,
    rs2_s,
    rs2_r,
):
    devices = pool * tensor
    rows, width = hidden_ref.shape
    requests = devices * rows
    half = tensor * rows
    block = width // tensor
    head_dim = query_gain_ref.shape[1]
    query_cols = qw.shape[1]
    key_cols = kvw.shape[0] // 2
    heads_here = query_cols // head_dim
    head_count = devices * heads_here
    kv_count = devices * key_cols // head_dim
    per_kv = devices // kv_count
    group = head_count // kv_count
    hidden_units = gw.shape[0]
    pieces = heads_here + 2
    span = 2 * SLOTS
    p = lax.axis_index("pool")
    t = lax.axis_index("tensor")
    me = p * tensor + t
    partner = {"pool": 1 - p, "tensor": t}

    barrier = pltpu.get_barrier_semaphore()

    def place(index):
        return {"pool": lax.div(index, tensor), "tensor": lax.rem(index, tensor)}

    for j in range(1, devices):
        pl.semaphore_signal(
            barrier, inc=1, device_id=place(lax.rem(me + j, devices)), device_id_type=MESH
        )

    smalls = [
        pltpu.make_async_copy(a, b, small_sem.at[i])
        for i, (a, b) in enumerate(
            [
                (hidden_hbm, hidden_ref),
                (slot_hbm, slot_ref),
                (length_hbm, length_ref),
                (input_gain_hbm, input_gain_ref),
                (frequency_hbm, frequency_ref),
                (query_gain_hbm, query_gain_ref),
                (key_gain_hbm, key_gain_ref),
                (post_gain_hbm, post_gain_ref),
            ]
        )
    ]
    for load in smalls:
        load.start()

    loads = [
        pltpu.make_async_copy(a, b, load_sem.at[i])
        for i, (a, b) in enumerate(
            [
                (qw_hbm, qw),
                (kw_hbm, kvw.at[:key_cols]),
                (vw_hbm, kvw.at[key_cols:]),
                (kc_hbm, kc),
                (vc_hbm, vc),
                (ow_hbm, ow),
                (gw_hbm, gw),
                (uw_hbm, uw),
                (dw_hbm, dw),
            ]
        )
    ]

    def flip(j):
        out, bit = 0, 1
        while bit < tensor:
            digit = lax.rem(lax.div(t, bit), 2)
            out = out + bit * (1 - digit if (j // bit) % 2 else digit)
            bit *= 2
        return out

    around = range(1, tensor)
    spin = [lax.rem(t + j, tensor) for j in range(tensor)]
    if tensor == 8:
        deep, side = lax.div(t, 2), lax.rem(t, 2)
        upper = lax.div(deep, 2)
        layers = [deep, deep + 1 - 2 * lax.rem(deep, 2), 2 - upper, 3 - 3 * upper]
        near = [2 * layer + q for layer in layers for q in (side, 1 - side)]
    else:
        near = [flip(j) for j in range(tensor)]

    def remote(source, target, sent, received, where):
        return pltpu.make_async_remote_copy(
            src_ref=source,
            dst_ref=target,
            send_sem=sent,
            recv_sem=received,
            device_id=where,
            device_id_type=MESH,
        )

    def in_plane(other):
        return {"pool": p, "tensor": other}

    class Gather:
        def __init__(self, buffer, sent, received):
            self.buffer, self.sent, self.received = buffer, sent, received

        def slot(self, q, index, k, where):
            at = self.buffer.at[q, index]
            return remote(at, at, self.sent.at[k], self.received.at[q, index], where)

        def send(self):
            for j in around:
                self.slot(p, t, j, in_plane(near[j])).start()
            self.slot(p, t, 0, partner).start()

        def forward(self, j):
            self.slot(p, near[j], tensor + j, partner).wait_recv()
            self.slot(p, near[j], tensor + j, partner).start()

        def across(self, j):
            self.slot(1 - p, near[j], 0, partner).wait_recv()

        def finish(self):
            self.slot(p, t, 0, partner).wait_send()
            for j in around:
                self.slot(p, t, j, in_plane(near[j])).wait_send()
                self.slot(p, near[j], tensor + j, partner).wait_send()

    first = Gather(ag1, ag1_s, ag1_r)
    second = Gather(mb, ag2_s, ag2_r)

    def hidden_copy(j, index):
        lanes = pl.ds(pl.multiple_of(near[j] * block, block), block)
        return remote(
            hidden_ref.at[:, lanes], hid.at[index], hid_s.at[j], hid_r.at[index], in_plane(near[j])
        )

    for load in smalls:
        load.wait()
    for load in loads:
        load.start()
    hidden = hidden_ref[...].astype(F32)
    ag1[p, t] = rms_scale(hidden, input_gain_ref[...]).astype(BF16)

    slot_row = slot_ref[...]
    length_row = length_ref[...]

    def iota(shape, dim):
        return lax.broadcasted_iota(jnp.int32, shape, dim)

    def hot(mask):
        return mask.astype(F32).astype(BF16)

    spread = hot(iota((requests, pieces * requests), 0) == lax.rem(iota((requests, pieces * requests), 1), requests))
    slot_wide = jnp.broadcast_to(slot_row, (span, requests))
    slot_tiled = jnp.dot(
        slot_wide.astype(F32).astype(BF16), spread, preferred_element_type=F32
    ).astype(jnp.int32)[:1]
    tall = devices * pieces * SLOTS
    row = iota((tall, pieces * requests), 0)
    col = iota((tall, pieces * requests), 1)
    wanted = lax.div(row, pieces * SLOTS) * SLOTS + lax.rem(row, SLOTS)
    scatter_hot = hot(
        (lax.rem(lax.div(row, SLOTS), pieces) == lax.div(col, requests)) & (wanted == slot_tiled)
    )
    eye = iota((requests, requests), 0) == iota((requests, requests), 1)
    slot_col = jnp.sum(
        jnp.where(eye, jnp.broadcast_to(slot_row, (requests, requests)), 0).astype(F32),
        axis=1,
        keepdims=True,
    ).astype(jnp.int32)
    home = devices * heads_here * SLOTS
    col = iota((requests, home), 1)
    held = lax.div(col, heads_here * SLOTS) * SLOTS + lax.rem(col, SLOTS)
    which = lax.rem(lax.div(col, SLOTS), heads_here)
    gather_hot = jnp.concatenate(
        [hot((which == i) & (held == slot_col)) for i in range(heads_here)], axis=0
    )
    place_id = lax.rem(iota((span, requests), 0), SLOTS)
    length_wide = jnp.broadcast_to(length_row, (span, requests)).astype(F32)
    base = me * SLOTS
    slot_length = jnp.sum(
        jnp.where(slot_wide == base + place_id, length_wide, 0.0), axis=1, keepdims=True
    )
    slot_offset = jnp.sum(
        jnp.where((slot_wide >= base) & (slot_wide < base + place_id), length_wide, 0.0),
        axis=1,
        keepdims=True,
    )
    angles = slot_length * frequency_ref[...]
    cosine = jnp.cos(angles)
    lane = iota((span, head_dim), 1)
    sine_part = jnp.where(lane < head_dim // 2, -jnp.sin(angles), jnp.sin(angles))
    pool_tokens = kc.shape[0]
    token = iota((span, pool_tokens), 1).astype(F32)
    inside = jnp.where((token >= slot_offset) & (token < slot_offset + slot_length), 1.0, 0.0)

    def turn(values, scale, copies):
        scaled = rms_scale(values, scale)
        return scaled * jnp.tile(cosine, (copies, 1)) + pltpu.roll(
            scaled, head_dim // 2, 1
        ) * jnp.tile(sine_part, (copies, 1))

    def turned(left, weight):
        return lax.dot_general(left, weight, (((1,), (1,)), ((), ())), preferred_element_type=F32)

    pl.semaphore_wait(barrier, devices - 1)
    first.send()
    for j in around:
        hidden_copy(j, t).start()
    hid[t] = hidden_ref[:, pl.ds(pl.multiple_of(t * block, block), block)]
    for load in loads[:3]:
        load.wait()
    for j in around:
        first.forward(j)
    for index in range(tensor):
        xs[p, index * rows : (index + 1) * rows, :] = ag1[p, index].astype(F32)
    for j in range(tensor):
        first.across(j)
    for index in range(tensor):
        xs[1 - p, index * rows : (index + 1) * rows, :] = ag1[1 - p, index].astype(F32)

    left = jnp.concatenate([xs[q] for q in range(pool)], axis=0).astype(BF16)
    query_part = jnp.dot(left, qw[...], preferred_element_type=F32).astype(BF16)
    kv_part = turned(left, kvw[...]).astype(BF16)

    wide = iota((2 * key_cols, 2 * head_dim), 1)
    tall = iota((2 * key_cols, 2 * head_dim), 0)
    shift = lax.rem(me, per_kv) * key_cols
    aim = jnp.where(tall < key_cols, tall + shift, tall - key_cols + head_dim + shift)
    kv_wide = jnp.dot(kv_part, hot(aim == wide), preferred_element_type=F32).astype(BF16)
    stacked = jnp.concatenate(
        [query_part[:, i * head_dim : (i + 1) * head_dim] for i in range(heads_here)]
        + [kv_wide[:, :head_dim], kv_wide[:, head_dim:]],
        axis=0,
    )
    slots = jnp.dot(scatter_hot, stacked, preferred_element_type=F32).astype(BF16)
    deep = pieces * SLOTS
    for index in range(devices):
        to_owner[index] = slots[index * deep : (index + 1) * deep]

    own_group, own_seat = lax.div(me, per_kv), lax.rem(me, per_kv)
    side_groups = kv_count // pool
    depth = lax.rem(own_group, side_groups)
    turns = [(0, 0)] + [(q, h) for q in (0, 1) for h in range(1, side_groups)] + [(1, 0)]
    groups = [
        (p if q == 0 else 1 - p) * side_groups + lax.rem(depth + h, side_groups) for q, h in turns
    ]

    def members(g):
        if g == 0:
            return [(j, groups[0] * per_kv + lax.rem(own_seat + j, per_kv)) for j in range(1, per_kv)]
        return [(g * per_kv + j, groups[g] * per_kv + j) for j in range(per_kv)]

    everyone = [member for g in range(kv_count) for member in members(g)]

    def post(outgoing, incoming, sent, received, number, peer):
        return remote(
            outgoing.at[peer], incoming.at[me], sent.at[number], received.at[me], place(peer)
        )

    def arrival(outgoing, incoming, sent, received, number, peer):
        return remote(
            outgoing.at[peer], incoming.at[peer], sent.at[number], received.at[peer], place(peer)
        )

    one = (to_owner, at_owner, a1_s, a1_r)
    two = (to_home, at_home, a2_s, a2_r)
    for member in everyone:
        post(*one, *member).start()
    at_owner[me] = to_owner[me]

    for j in around:
        hidden_copy(j, near[j]).wait_recv()
    for index in range(tensor):
        hblock[index * rows : (index + 1) * rows, :] = hid[index].astype(F32)
    for load in loads[3:5]:
        load.wait()

    scale_factor = 1.0 / math.sqrt(head_dim)
    copies = group * SLOTS // span
    allowed = jnp.tile(inside, (copies, 1)) > 0.5
    upper = iota((span, head_dim), 0) < SLOTS
    deep = heads_here * SLOTS
    for g in range(kv_count):
        for member in members(g):
            arrival(*one, *member).wait_recv()
        k = groups[g]
        blocks = [at_owner[k * per_kv + j].astype(F32) for j in range(per_kv)]
        query = jnp.concatenate([b[:deep] for b in blocks], axis=0)
        both = blocks[0][deep:]
        for b in blocks[1:]:
            both = both + b[deep:]
        turned_over = pltpu.roll(both, SLOTS, 0)
        key_new = turn(jnp.where(upper, both, turned_over), key_gain_ref[...], 1)
        own_value = jnp.tile(jnp.where(upper, turned_over, both), (copies, 1))
        own_key = jnp.tile(key_new.astype(BF16).astype(F32), (copies, 1))
        query = turn(query, query_gain_ref[...], copies).astype(BF16)
        lanes = pl.ds(pl.multiple_of(k * head_dim, head_dim), head_dim)
        scores = turned(query, kc[:, lanes]) * scale_factor
        own_score = jnp.sum(query.astype(F32) * own_key, axis=1, keepdims=True) * scale_factor
        scores = jnp.where(allowed, scores, -1e30)
        largest = jnp.maximum(jnp.max(scores, axis=1, keepdims=True), own_score)
        weights = jnp.exp(scores - largest)
        own_weight = jnp.exp(own_score - largest)
        denominator = jnp.sum(weights, axis=1, keepdims=True) + own_weight
        summed = jnp.dot(weights.astype(BF16), vc[:, lanes], preferred_element_type=F32)
        summed = summed + own_weight.astype(BF16).astype(F32) * own_value
        head_out = summed / denominator
        for j in range(per_kv):
            to_home[k * per_kv + j] = head_out[j * deep : (j + 1) * deep]
        for member in members(g):
            post(*two, *member).start()
    at_home[me] = to_home[me]

    loads[5].wait()
    for member in everyone:
        arrival(*two, *member).wait_recv()
    back = jnp.concatenate([at_home[index] for index in range(devices)], axis=0).astype(BF16)
    gathered = jnp.dot(gather_hot, back, preferred_element_type=F32).astype(BF16)
    head_rows = jnp.concatenate(
        [gathered[i * requests : (i + 1) * requests] for i in range(heads_here)], axis=1
    )

    pairs = tensor // 2
    wide = 2 * block

    def swap(part, peer, sent, received, c):
        return remote(part.at[c, 1 - p], peer.at[c], sent.at[c], received.at[c], partner)

    def products(left, weight, part, peer, sent, received, order):
        wide = part.shape[-1]
        for c in range(part.shape[0]):
            at = pl.ds(pl.multiple_of(order[c] * wide, wide), wide)
            product = jnp.dot(left, weight[:, at], preferred_element_type=F32)
            for q in range(pool):
                part[c, q] = product[q * half : (q + 1) * half].astype(BF16)
            swap(part, peer, sent, received, c).start()

    turn_of = [lax.rem(lax.div(t, 2) + 1 + c, pairs) for c in range(pairs)]
    products(head_rows, ow, part1, peer1, sw1_s, sw1_r, turn_of)

    def block_copy(k, other, slot):
        return remote(out1.at[other], in1.at[slot], rs1_s.at[k], rs1_r.at[slot], in_plane(other))

    for c in range(pairs):
        swap(part1, peer1, sw1_s, sw1_r, c).wait_recv()
        total = (peer1[c].astype(F32) + part1[c, p].astype(F32)).astype(BF16)
        for i in range(2):
            out1[2 * turn_of[c] + i] = total[:, i * block : (i + 1) * block]
        if c + 1 < pairs:
            for i in range(2):
                block_copy(2 * c + i, 2 * turn_of[c] + i, t).start()
    block_copy(tensor - 2, near[1], t).start()
    total = hblock[...] + out1[t].astype(F32)
    for j in around:
        block_copy(0, near[j], near[j]).wait_recv()
        total = total + in1[near[j]].astype(F32)
    mb[p, t] = total.astype(BF16)
    second.send()

    def part_of(j):
        at = pl.ds(pl.multiple_of(near[j] * block, block), block)
        values = jnp.concatenate([mb[q, near[j]] for q in range(pool)], axis=0).astype(F32)
        squares = values * values
        some = squares[:, :128]
        for i in range(1, block // 128):
            some = some + squares[:, i * 128 : (i + 1) * 128]
        scaled = (values * post_gain_ref[:, at]).astype(BF16)
        return some, turned(scaled, gw[:, at]), turned(scaled, uw[:, at])

    loads[6].wait()
    loads[7].wait()
    lead = 2
    sent_up_to = 0
    acc = None
    for j in range(tensor):
        while sent_up_to < min(j + lead, tensor - 1) and j > 0 or sent_up_to < j:
            sent_up_to += 1
            second.forward(sent_up_to)
        second.across(j)
        new = part_of(j)
        acc = new if acc is None else tuple(a + b for a, b in zip(acc, new))
    square, gate_part, up_part = acc
    mean = jnp.sum(square, axis=1, keepdims=True) * (1.0 / width)
    scale = lax.rsqrt(mean + eps)
    gate_part = gate_part * scale
    up_part = up_part * scale
    activated = (gate_part / (1.0 + jnp.exp(-gate_part)) * up_part).astype(BF16)

    loads[8].wait()
    cuts = part2.shape[0]
    wide = width // cuts
    products(activated, dw, part2, peer2, sw2_s, sw2_r, list(range(cuts)))

    def row_copy(j, slot):
        return remote(
            out2.at[spin[j]], in2.at[slot], rs2_s.at[j], rs2_r.at[slot], in_plane(spin[j])
        )

    for c in range(cuts):
        lanes = slice(c * wide, (c + 1) * wide)
        swap(part2, peer2, sw2_s, sw2_r, c).wait_recv()
        sum2[:, lanes] = peer2[c].astype(F32) + part2[c, p].astype(F32)
        for index in range(tensor):
            out2[index, :, lanes] = sum2[index * rows : (index + 1) * rows, lanes].astype(BF16)
    for j in around:
        row_copy(j, t).start()

    pick = hot(iota((8, requests), 1) == me * rows + iota((8, requests), 0))
    mixed_ref[...] = jnp.concatenate(
        [
            jnp.dot(
                pick,
                jnp.concatenate([mb[q, index] for q in range(pool)], axis=0),
                preferred_element_type=F32,
            )[:rows]
            for index in range(tensor)
        ],
        axis=1,
    )
    first.finish()
    for member in everyone:
        post(*one, *member).wait_send()
        post(*two, *member).wait_send()
    second.finish()
    for j in around:
        hidden_copy(j, t).wait_send()
    for c in range(pairs):
        swap(part1, peer1, sw1_s, sw1_r, c).wait_send()
    for c in range(cuts):
        swap(part2, peer2, sw2_s, sw2_r, c).wait_send()
    for c in range(pairs - 1):
        for i in range(2):
            block_copy(2 * c + i, 2 * turn_of[c] + i, t).wait_send()
    block_copy(tensor - 2, near[1], t).wait_send()

    total = out2[t].astype(F32)
    for j in around:
        row_copy(j, spin[j]).wait_recv()
        total = total + in2[spin[j]].astype(F32)
    added_ref[...] = total
    for j in around:
        row_copy(j, t).wait_send()


def fused(pool, tensor, *operands):
    (
        hidden,
        input_gain,
        query_weight,
        key_weight,
        value_weight,
        query_gain,
        key_gain,
        output_weight,
        post_gain,
        gate_weight,
        up_weight,
        down_weight,
        key_cache,
        value_cache,
        lengths,
        request_slot,
    ) = operands
    devices = pool * tensor
    rows, width = hidden.shape
    head_dim = query_gain.shape[0]
    query_cols = query_weight.shape[1]
    key_cols = key_weight.shape[1]
    heads_here = query_cols // head_dim
    half = tensor * rows
    block = width // tensor
    pairs = tensor // 2
    half_width = head_dim // 2
    frequency = theta ** (-np.arange(half_width) * 2.0 / head_dim)
    frequency = np.concatenate([frequency, frequency])[None, :].astype(np.float32)
    gate_turned, up_turned = gate_weight.T, up_weight.T
    dma = pltpu.SemaphoreType.DMA
    deep = (heads_here + 2) * SLOTS
    small = (
        hidden,
        request_slot[None, :],
        lengths[None, :],
        input_gain[None, :],
        frequency,
        query_gain[None, :],
        key_gain[None, :],
        post_gain[None, :],
    )
    scratch = [pltpu.VMEM(v.shape, v.dtype) for v in small] + [
        pltpu.VMEM(query_weight.shape, BF16),
        pltpu.VMEM((2 * key_cols, width), BF16),
        pltpu.VMEM(output_weight.shape, BF16),
        pltpu.VMEM(gate_turned.shape, BF16),
        pltpu.VMEM(up_turned.shape, BF16),
        pltpu.VMEM(down_weight.shape, BF16),
        pltpu.VMEM(key_cache.shape, BF16),
        pltpu.VMEM(value_cache.shape, BF16),
        pltpu.VMEM((pool, tensor, rows, width), BF16),
        pltpu.VMEM((tensor, rows, block), BF16),
        pltpu.VMEM((half, block), F32),
        pltpu.VMEM((pool, half, width), F32),
        pltpu.VMEM((devices, deep, head_dim), BF16),
        pltpu.VMEM((devices, deep, head_dim), BF16),
        pltpu.VMEM((devices, heads_here * SLOTS, head_dim), F32),
        pltpu.VMEM((devices, heads_here * SLOTS, head_dim), F32),
        pltpu.VMEM((pairs, pool, half, 2 * block), BF16),
        pltpu.VMEM((pairs, half, 2 * block), BF16),
        pltpu.VMEM((tensor, half, block), BF16),
        pltpu.VMEM((tensor, half, block), BF16),
        pltpu.VMEM((pool, tensor, half, block), BF16),
        pltpu.VMEM((CUTS, pool, half, width // CUTS), BF16),
        pltpu.VMEM((CUTS, half, width // CUTS), BF16),
        pltpu.VMEM((half, width), F32),
        pltpu.VMEM((tensor, rows, width), BF16),
        pltpu.VMEM((tensor, rows, width), BF16),
        dma((len(small),)),
        dma((9,)),
        dma((2 * tensor,)),
        dma((pool, tensor)),
        dma((tensor,)),
        dma((tensor,)),
        dma((2 * tensor,)),
        dma((pool, tensor)),
        dma((devices,)),
        dma((devices,)),
        dma((devices,)),
        dma((devices,)),
        dma((pairs,)),
        dma((pairs,)),
        dma((tensor,)),
        dma((tensor,)),
        dma((CUTS,)),
        dma((CUTS,)),
        dma((tensor,)),
        dma((tensor,)),
    ]
    vmem = pl.BlockSpec(memory_space=pltpu.VMEM)
    hbm = pl.BlockSpec(memory_space=pl.ANY)
    row = pltpu.VMEM(hidden.shape, F32)
    mixed, added = pl.pallas_call(
        functools.partial(step_kernel, pool, tensor),
        out_shape=(row, row),
        in_specs=[hbm] * (len(small) + 9),
        out_specs=(vmem, vmem),
        scratch_shapes=scratch,
        compiler_params=pltpu.CompilerParams(
            collective_id=0, has_side_effects=True, vmem_limit_bytes=62 * 1024 * 1024
        ),
    )(
        *small,
        query_weight,
        key_weight.T,
        value_weight.T,
        output_weight,
        gate_turned,
        up_turned,
        down_weight,
        key_cache,
        value_cache,
    )
    return mixed.astype(hidden.dtype), (mixed + added).astype(hidden.dtype)


def dispatch(pool, tensor, *operands):
    rows, width = operands[0].shape
    query_cols = operands[2].shape[1]
    key_cols = operands[3].shape[1]
    head_dim = operands[5].shape[0]
    devices = pool * tensor
    lanes = width % (tensor * 128) == 0 and head_dim == 128
    paired = tensor >= 4 and tensor & (tensor - 1) == 0 and tensor * rows == 16
    heads = query_cols == 2 * head_dim and head_dim % key_cols == 0
    few = devices * SLOTS <= 256 and devices * rows * 4 % 128 == 0
    if pool == 2 and lanes and paired and heads and few:
        return fused(pool, tensor, *operands)
    return on_device(*operands)


def solution(mesh):
    placed = (
        P(("groups", "pool", "tensor"), None),
        P(),
        P(None, ("pool", "tensor")),
        P(None, ("pool", "tensor")),
        P(None, ("pool", "tensor")),
        P(),
        P(),
        P(("pool", "tensor"), None),
        P(),
        P(None, ("pool", "tensor")),
        P(None, ("pool", "tensor")),
        P(("pool", "tensor"), None),
        P(("groups", "pool", "tensor"), None),
        P(("groups", "pool", "tensor"), None),
        P("groups"),
        P("groups"),
    )
    return jax.shard_map(
        functools.partial(dispatch, mesh.shape["pool"], mesh.shape["tensor"]),
        mesh=mesh,
        in_specs=placed,
        out_specs=(P(("groups", "pool", "tensor"), None), P(("groups", "pool", "tensor"), None)),
        check_vma=False,
    )
```

```python
import functools
import math

import jax
import jax.numpy as jnp
import numpy as np
from jax import lax
from jax.experimental import pallas as pl
from jax.experimental.pallas import tpu as pltpu
from jax.sharding import PartitionSpec as P

SLOTS = 4


eps = 1e-06
theta = 1000000.0


def rms_scale(values, scales):
    values = values.astype(jnp.float32)
    return values * lax.rsqrt(jnp.mean(values * values, axis=-1, keepdims=True) + eps) * scales


def rotate(values, position):
    half_width = values.shape[-1] // 2
    frequency = theta ** (-jnp.arange(half_width, dtype=jnp.float32) * 2.0 / values.shape[-1])
    angles = position * frequency
    cosine = jnp.cos(angles)
    sine_part = jnp.sin(angles)
    front_half = values[..., :half_width]
    back_half = values[..., half_width:]
    return jnp.concatenate(
        [front_half * cosine - back_half * sine_part, back_half * cosine + front_half * sine_part],
        axis=-1,
    )


def on_device(
    hidden,
    input_gain,
    query_weight,
    key_weight,
    value_weight,
    query_gain,
    key_gain,
    output_weight,
    post_gain,
    gate_weight,
    up_weight,
    down_weight,
    key_cache,
    value_cache,
    lengths,
    request_slot,
):
    devices = lax.axis_size(("pool", "tensor"))
    device_index = lax.axis_index(("pool", "tensor"))
    local_rows = hidden.shape[0]
    query_cols = query_weight.shape[1]
    key_cols = key_weight.shape[1]
    width_sent = query_cols + 2 * key_cols
    head_dim = query_gain.shape[0]
    slot_count = SLOTS
    head_count = devices * query_cols // head_dim
    kv_count = devices * key_cols // head_dim
    group_size = head_count // kv_count
    normed = rms_scale(hidden, input_gain).astype(jnp.bfloat16)
    shard_rows = lax.all_gather(normed, ("pool", "tensor"), axis=0, tiled=True)
    query_part = jnp.dot(shard_rows, query_weight, preferred_element_type=jnp.float32)
    key_part = jnp.dot(shard_rows, key_weight, preferred_element_type=jnp.float32)
    value_part = jnp.dot(shard_rows, value_weight, preferred_element_type=jnp.float32)
    projected = jnp.concatenate([query_part, key_part, value_part], axis=1).astype(jnp.bfloat16)
    outgoing = (
        jnp.zeros((devices * slot_count, width_sent), jnp.bfloat16).at[request_slot].set(projected)
    )
    outgoing = outgoing.reshape(devices, slot_count, width_sent)
    arrived = lax.all_to_all(
        outgoing, ("pool", "tensor"), split_axis=0, concat_axis=2, tiled=True
    ).reshape(slot_count, devices, width_sent)
    query_full = arrived[:, :, :query_cols].reshape(slot_count, head_count, head_dim)
    key_full = arrived[:, :, query_cols : query_cols + key_cols].reshape(
        slot_count, kv_count, head_dim
    )
    value_new = arrived[:, :, query_cols + key_cols :].reshape(slot_count, kv_count, head_dim)
    slot_ids = device_index * slot_count + jnp.arange(slot_count, dtype=jnp.int32)
    matches = request_slot[None, :] == slot_ids[:, None]
    slot_length = jnp.sum(jnp.where(matches, lengths[None, :], 0), axis=1)
    owner_of = request_slot // slot_count
    within = request_slot % slot_count
    earlier = (owner_of[None, :] == device_index) & (
        within[None, :] < jnp.arange(slot_count, dtype=jnp.int32)[:, None]
    )
    slot_offset = jnp.sum(jnp.where(earlier, lengths[None, :], 0), axis=1)
    position = slot_length.astype(jnp.float32)[:, None, None]
    query_heads = rotate(rms_scale(query_full, query_gain), position).astype(jnp.bfloat16)
    query_heads = query_heads.reshape(slot_count, kv_count, group_size, head_dim)
    key_new = rotate(rms_scale(key_full, key_gain), position).astype(jnp.bfloat16)
    pool_tokens = key_cache.shape[0]
    cached_keys = key_cache.reshape(pool_tokens, kv_count, head_dim)
    cached_values = value_cache.reshape(pool_tokens, kv_count, head_dim)
    scale_factor = 1.0 / math.sqrt(head_dim)
    scores = (
        jnp.einsum("skgd,tkd->skgt", query_heads, cached_keys, preferred_element_type=jnp.float32)
        * scale_factor
    )
    own_score = (
        jnp.einsum("skgd,skd->skg", query_heads, key_new, preferred_element_type=jnp.float32)
        * scale_factor
    )
    token_pos = jnp.arange(pool_tokens, dtype=jnp.int32)
    inside = (token_pos[None, :] >= slot_offset[:, None]) & (
        token_pos[None, :] < (slot_offset + slot_length)[:, None]
    )
    inside = inside[:, None, None, :]
    largest = jnp.maximum(jnp.max(jnp.where(inside, scores, -1e30), axis=3), own_score)
    weights = jnp.where(inside, jnp.exp(scores - largest[..., None]), 0.0)
    own_weight = jnp.exp(own_score - largest)
    denominator = jnp.sum(weights, axis=3) + own_weight
    summed = jnp.einsum(
        "skgt,tkd->skgd",
        weights.astype(jnp.bfloat16),
        cached_values,
        preferred_element_type=jnp.float32,
    )
    own_low = own_weight.astype(jnp.bfloat16).astype(jnp.float32)
    summed = summed + own_low[..., None] * value_new.astype(jnp.float32)[:, :, None, :]
    head_out = (
        (summed / denominator[..., None])
        .astype(jnp.bfloat16)
        .reshape(slot_count, devices, query_cols)
    )
    returned = lax.all_to_all(head_out, ("pool", "tensor"), split_axis=1, concat_axis=0, tiled=True)
    head_rows = returned.reshape(devices * slot_count, query_cols)[request_slot]
    partial_value = jnp.dot(head_rows, output_weight, preferred_element_type=jnp.float32)
    row_start = device_index * local_rows
    own_part = lax.dynamic_slice_in_dim(partial_value, row_start, local_rows, 0) + hidden.astype(
        jnp.float32
    )
    partial_value = lax.dynamic_update_slice_in_dim(partial_value, own_part, row_start, 0)
    totals = lax.psum(partial_value, ("pool", "tensor"))
    mixed_all = totals.astype(jnp.bfloat16)
    mixed_rows = lax.dynamic_slice_in_dim(mixed_all, row_start, local_rows, 0)
    post_normed = rms_scale(mixed_all, post_gain).astype(jnp.bfloat16)
    gate_part = jnp.dot(post_normed, gate_weight, preferred_element_type=jnp.float32)
    up_part = jnp.dot(post_normed, up_weight, preferred_element_type=jnp.float32)
    activated = (jax.nn.silu(gate_part) * up_part).astype(jnp.bfloat16)
    lowered = lax.psum_scatter(
        jnp.dot(activated, down_weight, preferred_element_type=jnp.float32),
        ("pool", "tensor"),
        scatter_dimension=0,
        tiled=True,
    )
    final_rows = (mixed_rows.astype(jnp.float32) + lowered).astype(jnp.bfloat16)
    return (mixed_rows, final_rows)


MESH = pl.DeviceIdType.MESH
F32 = jnp.float32
BF16 = jnp.bfloat16
CUTS = 2


def step_kernel(
    pool,
    tensor,
    hidden_hbm,
    slot_hbm,
    length_hbm,
    input_gain_hbm,
    frequency_hbm,
    query_gain_hbm,
    key_gain_hbm,
    post_gain_hbm,
    qw_hbm,
    kw_hbm,
    vw_hbm,
    ow_hbm,
    gw_hbm,
    uw_hbm,
    dw_hbm,
    kc_hbm,
    vc_hbm,
    mixed_ref,
    added_ref,
    hidden_ref,
    slot_ref,
    length_ref,
    input_gain_ref,
    frequency_ref,
    query_gain_ref,
    key_gain_ref,
    post_gain_ref,
    qw,
    kvw,
    ow,
    gw,
    uw,
    dw,
    kc,
    vc,
    ag1,
    hid,
    hblock,
    xs,
    to_owner,
    at_owner,
    to_home,
    at_home,
    part1,
    peer1,
    out1,
    in1,
    mb,
    part2,
    peer2,
    sum2,
    out2,
    in2,
    small_sem,
    load_sem,
    ag1_s,
    ag1_r,
    hid_s,
    hid_r,
    ag2_s,
    ag2_r,
    a1_s,
    a1_r,
    a2_s,
    a2_r,
    sw1_s,
    sw1_r,
    rs1_s,
    rs1_r,
    sw2_s,
    sw2_r,
    rs2_s,
    rs2_r,
):
    devices = pool * tensor
    rows, width = hidden_ref.shape
    requests = devices * rows
    half = tensor * rows
    block = width // tensor
    head_dim = query_gain_ref.shape[1]
    query_cols = qw.shape[1]
    key_cols = kvw.shape[0] // 2
    heads_here = query_cols // head_dim
    head_count = devices * heads_here
    kv_count = devices * key_cols // head_dim
    per_kv = devices // kv_count
    group = head_count // kv_count
    hidden_units = gw.shape[0]
    pieces = heads_here + 2
    span = 2 * SLOTS
    p = lax.axis_index("pool")
    t = lax.axis_index("tensor")
    me = p * tensor + t
    partner = {"pool": 1 - p, "tensor": t}

    barrier = pltpu.get_barrier_semaphore()

    def place(index):
        return {"pool": lax.div(index, tensor), "tensor": lax.rem(index, tensor)}

    for j in range(1, devices):
        pl.semaphore_signal(
            barrier, inc=1, device_id=place(lax.rem(me + j, devices)), device_id_type=MESH
        )

    smalls = [
        pltpu.make_async_copy(a, b, small_sem.at[i])
        for i, (a, b) in enumerate(
            [
                (hidden_hbm, hidden_ref),
                (slot_hbm, slot_ref),
                (length_hbm, length_ref),
                (input_gain_hbm, input_gain_ref),
                (frequency_hbm, frequency_ref),
                (query_gain_hbm, query_gain_ref),
                (key_gain_hbm, key_gain_ref),
                (post_gain_hbm, post_gain_ref),
            ]
        )
    ]
    for load in smalls:
        load.start()

    loads = [
        pltpu.make_async_copy(a, b, load_sem.at[i])
        for i, (a, b) in enumerate(
            [
                (qw_hbm, qw),
                (kw_hbm, kvw.at[:key_cols]),
                (vw_hbm, kvw.at[key_cols:]),
                (kc_hbm, kc),
                (vc_hbm, vc),
                (ow_hbm, ow),
                (gw_hbm, gw),
                (uw_hbm, uw),
                (dw_hbm, dw),
            ]
        )
    ]

    def flip(j):
        out, bit = 0, 1
        while bit < tensor:
            digit = lax.rem(lax.div(t, bit), 2)
            out = out + bit * (1 - digit if (j // bit) % 2 else digit)
            bit *= 2
        return out

    around = range(1, tensor)
    spin = [lax.rem(t + j, tensor) for j in range(tensor)]
    if tensor == 8:
        deep, side = lax.div(t, 2), lax.rem(t, 2)
        upper = lax.div(deep, 2)
        layers = [deep, deep + 1 - 2 * lax.rem(deep, 2), 2 - upper, 3 - 3 * upper]
        near = [2 * layer + q for layer in layers for q in (side, 1 - side)]
    else:
        near = [flip(j) for j in range(tensor)]

    def remote(source, target, sent, received, where):
        return pltpu.make_async_remote_copy(
            src_ref=source,
            dst_ref=target,
            send_sem=sent,
            recv_sem=received,
            device_id=where,
            device_id_type=MESH,
        )

    def in_plane(other):
        return {"pool": p, "tensor": other}

    class Gather:
        def __init__(self, buffer, sent, received, order):
            self.buffer, self.sent, self.received, self.order = buffer, sent, received, order

        def slot(self, q, index, k, where):
            at = self.buffer.at[q, index]
            return remote(at, at, self.sent.at[k], self.received.at[q, index], where)

        def send(self):
            self.slot(p, t, 0, partner).start()
            for j in around:
                self.slot(p, t, j, in_plane(self.order[j])).start()

        def forward(self, j):
            self.slot(p, near[j], tensor + j, partner).wait_recv()
            self.slot(p, near[j], tensor + j, partner).start()

        def across(self, j):
            self.slot(1 - p, near[j], 0, partner).wait_recv()

        def finish(self):
            self.slot(p, t, 0, partner).wait_send()
            for j in around:
                self.slot(p, t, j, in_plane(self.order[j])).wait_send()
                self.slot(p, near[j], tensor + j, partner).wait_send()

    first = Gather(ag1, ag1_s, ag1_r, spin)
    second = Gather(mb, ag2_s, ag2_r, near)

    def hidden_copy(j, index):
        lanes = pl.ds(pl.multiple_of(near[j] * block, block), block)
        return remote(
            hidden_ref.at[:, lanes], hid.at[index], hid_s.at[j], hid_r.at[index], in_plane(near[j])
        )

    for load in smalls:
        load.wait()
    for load in loads:
        load.start()
    hidden = hidden_ref[...].astype(F32)
    ag1[p, t] = rms_scale(hidden, input_gain_ref[...]).astype(BF16)

    slot_row = slot_ref[...]
    length_row = length_ref[...]

    def iota(shape, dim):
        return lax.broadcasted_iota(jnp.int32, shape, dim)

    def hot(mask):
        return mask.astype(F32).astype(BF16)

    spread = hot(iota((requests, pieces * requests), 0) == lax.rem(iota((requests, pieces * requests), 1), requests))
    slot_wide = jnp.broadcast_to(slot_row, (span, requests))
    slot_tiled = jnp.dot(
        slot_wide.astype(F32).astype(BF16), spread, preferred_element_type=F32
    ).astype(jnp.int32)[:1]
    tall = devices * pieces * SLOTS
    row = iota((tall, pieces * requests), 0)
    col = iota((tall, pieces * requests), 1)
    wanted = lax.div(row, pieces * SLOTS) * SLOTS + lax.rem(row, SLOTS)
    scatter_hot = hot(
        (lax.rem(lax.div(row, SLOTS), pieces) == lax.div(col, requests)) & (wanted == slot_tiled)
    )
    eye = iota((requests, requests), 0) == iota((requests, requests), 1)
    slot_col = jnp.sum(
        jnp.where(eye, jnp.broadcast_to(slot_row, (requests, requests)), 0).astype(F32),
        axis=1,
        keepdims=True,
    ).astype(jnp.int32)
    home = devices * heads_here * SLOTS
    col = iota((requests, home), 1)
    held = lax.div(col, heads_here * SLOTS) * SLOTS + lax.rem(col, SLOTS)
    which = lax.rem(lax.div(col, SLOTS), heads_here)
    gather_hot = jnp.concatenate(
        [hot((which == i) & (held == slot_col)) for i in range(heads_here)], axis=0
    )
    place_id = lax.rem(iota((span, requests), 0), SLOTS)
    length_wide = jnp.broadcast_to(length_row, (span, requests)).astype(F32)
    base = me * SLOTS
    slot_length = jnp.sum(
        jnp.where(slot_wide == base + place_id, length_wide, 0.0), axis=1, keepdims=True
    )
    slot_offset = jnp.sum(
        jnp.where((slot_wide >= base) & (slot_wide < base + place_id), length_wide, 0.0),
        axis=1,
        keepdims=True,
    )
    angles = slot_length * frequency_ref[...]
    cosine = jnp.cos(angles)
    lane = iota((span, head_dim), 1)
    sine_part = jnp.where(lane < head_dim // 2, -jnp.sin(angles), jnp.sin(angles))
    pool_tokens = kc.shape[0]
    token = iota((span, pool_tokens), 1).astype(F32)
    inside = jnp.where((token >= slot_offset) & (token < slot_offset + slot_length), 1.0, 0.0)

    def turn(values, scale, copies):
        scaled = rms_scale(values, scale)
        return scaled * jnp.tile(cosine, (copies, 1)) + pltpu.roll(
            scaled, head_dim // 2, 1
        ) * jnp.tile(sine_part, (copies, 1))

    def turned(left, weight):
        return lax.dot_general(left, weight, (((1,), (1,)), ((), ())), preferred_element_type=F32)

    pl.semaphore_wait(barrier, devices - 1)
    first.send()
    hid[t] = hidden_ref[:, pl.ds(pl.multiple_of(t * block, block), block)]
    for load in loads[:3]:
        load.wait()
    for j in around:
        first.forward(j)
    for j in around:
        hidden_copy(j, t).start()
    for index in range(tensor):
        xs[p, index * rows : (index + 1) * rows, :] = ag1[p, index].astype(F32)
    for j in range(tensor):
        first.across(j)
    for index in range(tensor):
        xs[1 - p, index * rows : (index + 1) * rows, :] = ag1[1 - p, index].astype(F32)

    left = jnp.concatenate([xs[q] for q in range(pool)], axis=0).astype(BF16)
    query_part = jnp.dot(left, qw[...], preferred_element_type=F32).astype(BF16)
    kv_part = turned(left, kvw[...]).astype(BF16)

    wide = iota((2 * key_cols, 2 * head_dim), 1)
    tall = iota((2 * key_cols, 2 * head_dim), 0)
    shift = lax.rem(me, per_kv) * key_cols
    aim = jnp.where(tall < key_cols, tall + shift, tall - key_cols + head_dim + shift)
    kv_wide = jnp.dot(kv_part, hot(aim == wide), preferred_element_type=F32).astype(BF16)
    stacked = jnp.concatenate(
        [query_part[:, i * head_dim : (i + 1) * head_dim] for i in range(heads_here)]
        + [kv_wide[:, :head_dim], kv_wide[:, head_dim:]],
        axis=0,
    )
    slots = jnp.dot(scatter_hot, stacked, preferred_element_type=F32).astype(BF16)
    deep = pieces * SLOTS
    for index in range(devices):
        to_owner[index] = slots[index * deep : (index + 1) * deep]

    own_group, own_seat = lax.div(me, per_kv), lax.rem(me, per_kv)
    side_groups = kv_count // pool
    depth = lax.rem(own_group, side_groups)
    turns = [(0, 0)] + [(q, h) for q in (0, 1) for h in range(1, side_groups)] + [(1, 0)]
    groups = [
        (p if q == 0 else 1 - p) * side_groups + lax.rem(depth + h, side_groups) for q, h in turns
    ]

    def members(g):
        if g == 0:
            return [(j, groups[0] * per_kv + lax.rem(own_seat + j, per_kv)) for j in range(1, per_kv)]
        return [
            (g * per_kv + j, groups[g] * per_kv + lax.rem(own_seat + j, per_kv))
            for j in range(per_kv)
        ]

    everyone = [member for g in range(kv_count) for member in members(g)]

    def post(outgoing, incoming, sent, received, number, peer):
        return remote(
            outgoing.at[peer], incoming.at[me], sent.at[number], received.at[me], place(peer)
        )

    def arrival(outgoing, incoming, sent, received, number, peer):
        return remote(
            outgoing.at[peer], incoming.at[peer], sent.at[number], received.at[peer], place(peer)
        )

    one = (to_owner, at_owner, a1_s, a1_r)
    two = (to_home, at_home, a2_s, a2_r)
    for member in everyone:
        post(*one, *member).start()
    at_owner[me] = to_owner[me]

    for j in around:
        hidden_copy(j, near[j]).wait_recv()
    for index in range(tensor):
        hblock[index * rows : (index + 1) * rows, :] = hid[index].astype(F32)
    for load in loads[3:5]:
        load.wait()

    scale_factor = 1.0 / math.sqrt(head_dim)
    copies = group * SLOTS // span
    allowed = jnp.tile(inside, (copies, 1)) > 0.5
    upper = iota((span, head_dim), 0) < SLOTS
    deep = heads_here * SLOTS
    for g in range(kv_count):
        for member in members(g):
            arrival(*one, *member).wait_recv()
        k = groups[g]
        blocks = [at_owner[k * per_kv + j].astype(F32) for j in range(per_kv)]
        query = jnp.concatenate([b[:deep] for b in blocks], axis=0)
        both = blocks[0][deep:]
        for b in blocks[1:]:
            both = both + b[deep:]
        turned_over = pltpu.roll(both, SLOTS, 0)
        key_new = turn(jnp.where(upper, both, turned_over), key_gain_ref[...], 1)
        own_value = jnp.tile(jnp.where(upper, turned_over, both), (copies, 1))
        own_key = jnp.tile(key_new.astype(BF16).astype(F32), (copies, 1))
        query = turn(query, query_gain_ref[...], copies).astype(BF16)
        lanes = pl.ds(pl.multiple_of(k * head_dim, head_dim), head_dim)
        scores = turned(query, kc[:, lanes]) * scale_factor
        own_score = jnp.sum(query.astype(F32) * own_key, axis=1, keepdims=True) * scale_factor
        scores = jnp.where(allowed, scores, -1e30)
        largest = jnp.maximum(jnp.max(scores, axis=1, keepdims=True), own_score)
        weights = jnp.exp(scores - largest)
        own_weight = jnp.exp(own_score - largest)
        denominator = jnp.sum(weights, axis=1, keepdims=True) + own_weight
        summed = jnp.dot(weights.astype(BF16), vc[:, lanes], preferred_element_type=F32)
        summed = summed + own_weight.astype(BF16).astype(F32) * own_value
        head_out = summed / denominator
        for j in range(per_kv):
            to_home[k * per_kv + j] = head_out[j * deep : (j + 1) * deep]
        for member in members(g):
            post(*two, *member).start()
    at_home[me] = to_home[me]

    loads[5].wait()
    for member in everyone:
        arrival(*two, *member).wait_recv()
    back = jnp.concatenate([at_home[index] for index in range(devices)], axis=0).astype(BF16)
    gathered = jnp.dot(gather_hot, back, preferred_element_type=F32).astype(BF16)
    head_rows = jnp.concatenate(
        [gathered[i * requests : (i + 1) * requests] for i in range(heads_here)], axis=1
    )

    pairs = tensor // 2
    wide = 2 * block

    def swap(part, peer, sent, received, c):
        return remote(part.at[c, 1 - p], peer.at[c], sent.at[c], received.at[c], partner)

    def products(left, weight, part, peer, sent, received, order):
        wide = part.shape[-1]
        for c in range(part.shape[0]):
            at = pl.ds(pl.multiple_of(order[c] * wide, wide), wide)
            product = jnp.dot(left, weight[:, at], preferred_element_type=F32)
            for q in range(pool):
                part[c, q] = product[q * half : (q + 1) * half].astype(BF16)
            swap(part, peer, sent, received, c).start()

    turn_of = [lax.rem(lax.div(t, 2) + 1 + c, pairs) for c in range(pairs)]
    products(head_rows, ow, part1, peer1, sw1_s, sw1_r, turn_of)

    def block_copy(k, other, slot):
        return remote(out1.at[other], in1.at[slot], rs1_s.at[k], rs1_r.at[slot], in_plane(other))

    for c in range(pairs):
        swap(part1, peer1, sw1_s, sw1_r, c).wait_recv()
        total = (peer1[c].astype(F32) + part1[c, p].astype(F32)).astype(BF16)
        for i in range(2):
            out1[2 * turn_of[c] + i] = total[:, i * block : (i + 1) * block]
        if c + 1 < pairs:
            for i in range(2):
                block_copy(2 * c + i, 2 * turn_of[c] + i, t).start()
    block_copy(tensor - 2, near[1], t).start()
    total = hblock[...] + out1[t].astype(F32)
    for j in around:
        block_copy(0, near[j], near[j]).wait_recv()
        total = total + in1[near[j]].astype(F32)
    mb[p, t] = total.astype(BF16)
    second.send()

    def part_of(j):
        at = pl.ds(pl.multiple_of(near[j] * block, block), block)
        values = jnp.concatenate([mb[q, near[j]] for q in range(pool)], axis=0).astype(F32)
        squares = values * values
        some = squares[:, :128]
        for i in range(1, block // 128):
            some = some + squares[:, i * 128 : (i + 1) * 128]
        scaled = (values * post_gain_ref[:, at]).astype(BF16)
        return some, turned(scaled, gw[:, at]), turned(scaled, uw[:, at])

    loads[6].wait()
    loads[7].wait()
    lead = 2
    sent_up_to = 0
    acc = None
    for j in range(tensor):
        while sent_up_to < min(j + lead, tensor - 1) and j > 0 or sent_up_to < j:
            sent_up_to += 1
            second.forward(sent_up_to)
        second.across(j)
        new = part_of(j)
        acc = new if acc is None else tuple(a + b for a, b in zip(acc, new))
    square, gate_part, up_part = acc
    mean = jnp.sum(square, axis=1, keepdims=True) * (1.0 / width)
    scale = lax.rsqrt(mean + eps)
    gate_part = gate_part * scale
    up_part = up_part * scale
    activated = (gate_part / (1.0 + jnp.exp(-gate_part)) * up_part).astype(BF16)

    loads[8].wait()
    cuts = part2.shape[0]
    wide = width // cuts
    products(activated, dw, part2, peer2, sw2_s, sw2_r, list(range(cuts)))

    def row_copy(j, slot):
        return remote(
            out2.at[spin[j]], in2.at[slot], rs2_s.at[j], rs2_r.at[slot], in_plane(spin[j])
        )

    for c in range(cuts):
        lanes = slice(c * wide, (c + 1) * wide)
        swap(part2, peer2, sw2_s, sw2_r, c).wait_recv()
        sum2[:, lanes] = peer2[c].astype(F32) + part2[c, p].astype(F32)
        for index in range(tensor):
            out2[index, :, lanes] = sum2[index * rows : (index + 1) * rows, lanes].astype(BF16)
    for j in around:
        row_copy(j, t).start()

    pick = hot(iota((8, requests), 1) == me * rows + iota((8, requests), 0))
    mixed_ref[...] = jnp.concatenate(
        [
            jnp.dot(
                pick,
                jnp.concatenate([mb[q, index] for q in range(pool)], axis=0),
                preferred_element_type=F32,
            )[:rows]
            for index in range(tensor)
        ],
        axis=1,
    )
    first.finish()
    for member in everyone:
        post(*one, *member).wait_send()
        post(*two, *member).wait_send()
    second.finish()
    for j in around:
        hidden_copy(j, t).wait_send()
    for c in range(pairs):
        swap(part1, peer1, sw1_s, sw1_r, c).wait_send()
    for c in range(cuts):
        swap(part2, peer2, sw2_s, sw2_r, c).wait_send()
    for c in range(pairs - 1):
        for i in range(2):
            block_copy(2 * c + i, 2 * turn_of[c] + i, t).wait_send()
    block_copy(tensor - 2, near[1], t).wait_send()

    total = out2[t].astype(F32)
    for j in around:
        row_copy(j, spin[j]).wait_recv()
        total = total + in2[spin[j]].astype(F32)
    added_ref[...] = total
    for j in around:
        row_copy(j, t).wait_send()


def fused(pool, tensor, *operands):
    (
        hidden,
        input_gain,
        query_weight,
        key_weight,
        value_weight,
        query_gain,
        key_gain,
        output_weight,
        post_gain,
        gate_weight,
        up_weight,
        down_weight,
        key_cache,
        value_cache,
        lengths,
        request_slot,
    ) = operands
    devices = pool * tensor
    rows, width = hidden.shape
    head_dim = query_gain.shape[0]
    query_cols = query_weight.shape[1]
    key_cols = key_weight.shape[1]
    heads_here = query_cols // head_dim
    half = tensor * rows
    block = width // tensor
    pairs = tensor // 2
    half_width = head_dim // 2
    frequency = theta ** (-np.arange(half_width) * 2.0 / head_dim)
    frequency = np.concatenate([frequency, frequency])[None, :].astype(np.float32)
    gate_turned, up_turned = gate_weight.T, up_weight.T
    dma = pltpu.SemaphoreType.DMA
    deep = (heads_here + 2) * SLOTS
    small = (
        hidden,
        request_slot[None, :],
        lengths[None, :],
        input_gain[None, :],
        frequency,
        query_gain[None, :],
        key_gain[None, :],
        post_gain[None, :],
    )
    scratch = [pltpu.VMEM(v.shape, v.dtype) for v in small] + [
        pltpu.VMEM(query_weight.shape, BF16),
        pltpu.VMEM((2 * key_cols, width), BF16),
        pltpu.VMEM(output_weight.shape, BF16),
        pltpu.VMEM(gate_turned.shape, BF16),
        pltpu.VMEM(up_turned.shape, BF16),
        pltpu.VMEM(down_weight.shape, BF16),
        pltpu.VMEM(key_cache.shape, BF16),
        pltpu.VMEM(value_cache.shape, BF16),
        pltpu.VMEM((pool, tensor, rows, width), BF16),
        pltpu.VMEM((tensor, rows, block), BF16),
        pltpu.VMEM((half, block), F32),
        pltpu.VMEM((pool, half, width), F32),
        pltpu.VMEM((devices, deep, head_dim), BF16),
        pltpu.VMEM((devices, deep, head_dim), BF16),
        pltpu.VMEM((devices, heads_here * SLOTS, head_dim), F32),
        pltpu.VMEM((devices, heads_here * SLOTS, head_dim), F32),
        pltpu.VMEM((pairs, pool, half, 2 * block), BF16),
        pltpu.VMEM((pairs, half, 2 * block), BF16),
        pltpu.VMEM((tensor, half, block), BF16),
        pltpu.VMEM((tensor, half, block), BF16),
        pltpu.VMEM((pool, tensor, half, block), BF16),
        pltpu.VMEM((CUTS, pool, half, width // CUTS), BF16),
        pltpu.VMEM((CUTS, half, width // CUTS), BF16),
        pltpu.VMEM((half, width), F32),
        pltpu.VMEM((tensor, rows, width), BF16),
        pltpu.VMEM((tensor, rows, width), BF16),
        dma((len(small),)),
        dma((9,)),
        dma((2 * tensor,)),
        dma((pool, tensor)),
        dma((tensor,)),
        dma((tensor,)),
        dma((2 * tensor,)),
        dma((pool, tensor)),
        dma((devices,)),
        dma((devices,)),
        dma((devices,)),
        dma((devices,)),
        dma((pairs,)),
        dma((pairs,)),
        dma((tensor,)),
        dma((tensor,)),
        dma((CUTS,)),
        dma((CUTS,)),
        dma((tensor,)),
        dma((tensor,)),
    ]
    vmem = pl.BlockSpec(memory_space=pltpu.VMEM)
    hbm = pl.BlockSpec(memory_space=pl.ANY)
    row = pltpu.VMEM(hidden.shape, F32)
    mixed, added = pl.pallas_call(
        functools.partial(step_kernel, pool, tensor),
        out_shape=(row, row),
        in_specs=[hbm] * (len(small) + 9),
        out_specs=(vmem, vmem),
        scratch_shapes=scratch,
        compiler_params=pltpu.CompilerParams(
            collective_id=0, has_side_effects=True, vmem_limit_bytes=62 * 1024 * 1024
        ),
    )(
        *small,
        query_weight,
        key_weight.T,
        value_weight.T,
        output_weight,
        gate_turned,
        up_turned,
        down_weight,
        key_cache,
        value_cache,
    )
    return mixed.astype(hidden.dtype), (mixed + added).astype(hidden.dtype)


def dispatch(pool, tensor, *operands):
    rows, width = operands[0].shape
    query_cols = operands[2].shape[1]
    key_cols = operands[3].shape[1]
    head_dim = operands[5].shape[0]
    devices = pool * tensor
    lanes = width % (tensor * 128) == 0 and head_dim == 128
    paired = tensor >= 4 and tensor & (tensor - 1) == 0 and tensor * rows == 16
    heads = query_cols == 2 * head_dim and head_dim % key_cols == 0
    few = devices * SLOTS <= 256 and devices * rows * 4 % 128 == 0
    if pool == 2 and lanes and paired and heads and few:
        return fused(pool, tensor, *operands)
    return on_device(*operands)


def solution(mesh):
    placed = (
        P(("groups", "pool", "tensor"), None),
        P(),
        P(None, ("pool", "tensor")),
        P(None, ("pool", "tensor")),
        P(None, ("pool", "tensor")),
        P(),
        P(),
        P(("pool", "tensor"), None),
        P(),
        P(None, ("pool", "tensor")),
        P(None, ("pool", "tensor")),
        P(("pool", "tensor"), None),
        P(("groups", "pool", "tensor"), None),
        P(("groups", "pool", "tensor"), None),
        P("groups"),
        P("groups"),
    )
    return jax.shard_map(
        functools.partial(dispatch, mesh.shape["pool"], mesh.shape["tensor"]),
        mesh=mesh,
        in_specs=placed,
        out_specs=(P(("groups", "pool", "tensor"), None), P(("groups", "pool", "tensor"), None)),
        check_vma=False,
    )
```

```python
import functools
import math

import jax
import jax.numpy as jnp
import numpy as np
from jax import lax
from jax.experimental import pallas as pl
from jax.experimental.pallas import tpu as pltpu
from jax.sharding import PartitionSpec as P

SLOTS = 4


eps = 1e-06
theta = 1000000.0


def rms_scale(values, scales):
    values = values.astype(jnp.float32)
    return values * lax.rsqrt(jnp.mean(values * values, axis=-1, keepdims=True) + eps) * scales


def rotate(values, position):
    half_width = values.shape[-1] // 2
    frequency = theta ** (-jnp.arange(half_width, dtype=jnp.float32) * 2.0 / values.shape[-1])
    angles = position * frequency
    cosine = jnp.cos(angles)
    sine_part = jnp.sin(angles)
    front_half = values[..., :half_width]
    back_half = values[..., half_width:]
    return jnp.concatenate(
        [front_half * cosine - back_half * sine_part, back_half * cosine + front_half * sine_part],
        axis=-1,
    )


def on_device(
    hidden,
    input_gain,
    query_weight,
    key_weight,
    value_weight,
    query_gain,
    key_gain,
    output_weight,
    post_gain,
    gate_weight,
    up_weight,
    down_weight,
    key_cache,
    value_cache,
    lengths,
    request_slot,
):
    devices = lax.axis_size(("pool", "tensor"))
    device_index = lax.axis_index(("pool", "tensor"))
    local_rows = hidden.shape[0]
    query_cols = query_weight.shape[1]
    key_cols = key_weight.shape[1]
    width_sent = query_cols + 2 * key_cols
    head_dim = query_gain.shape[0]
    slot_count = SLOTS
    head_count = devices * query_cols // head_dim
    kv_count = devices * key_cols // head_dim
    group_size = head_count // kv_count
    normed = rms_scale(hidden, input_gain).astype(jnp.bfloat16)
    shard_rows = lax.all_gather(normed, ("pool", "tensor"), axis=0, tiled=True)
    query_part = jnp.dot(shard_rows, query_weight, preferred_element_type=jnp.float32)
    key_part = jnp.dot(shard_rows, key_weight, preferred_element_type=jnp.float32)
    value_part = jnp.dot(shard_rows, value_weight, preferred_element_type=jnp.float32)
    projected = jnp.concatenate([query_part, key_part, value_part], axis=1).astype(jnp.bfloat16)
    outgoing = (
        jnp.zeros((devices * slot_count, width_sent), jnp.bfloat16).at[request_slot].set(projected)
    )
    outgoing = outgoing.reshape(devices, slot_count, width_sent)
    arrived = lax.all_to_all(
        outgoing, ("pool", "tensor"), split_axis=0, concat_axis=2, tiled=True
    ).reshape(slot_count, devices, width_sent)
    query_full = arrived[:, :, :query_cols].reshape(slot_count, head_count, head_dim)
    key_full = arrived[:, :, query_cols : query_cols + key_cols].reshape(
        slot_count, kv_count, head_dim
    )
    value_new = arrived[:, :, query_cols + key_cols :].reshape(slot_count, kv_count, head_dim)
    slot_ids = device_index * slot_count + jnp.arange(slot_count, dtype=jnp.int32)
    matches = request_slot[None, :] == slot_ids[:, None]
    slot_length = jnp.sum(jnp.where(matches, lengths[None, :], 0), axis=1)
    owner_of = request_slot // slot_count
    within = request_slot % slot_count
    earlier = (owner_of[None, :] == device_index) & (
        within[None, :] < jnp.arange(slot_count, dtype=jnp.int32)[:, None]
    )
    slot_offset = jnp.sum(jnp.where(earlier, lengths[None, :], 0), axis=1)
    position = slot_length.astype(jnp.float32)[:, None, None]
    query_heads = rotate(rms_scale(query_full, query_gain), position).astype(jnp.bfloat16)
    query_heads = query_heads.reshape(slot_count, kv_count, group_size, head_dim)
    key_new = rotate(rms_scale(key_full, key_gain), position).astype(jnp.bfloat16)
    pool_tokens = key_cache.shape[0]
    cached_keys = key_cache.reshape(pool_tokens, kv_count, head_dim)
    cached_values = value_cache.reshape(pool_tokens, kv_count, head_dim)
    scale_factor = 1.0 / math.sqrt(head_dim)
    scores = (
        jnp.einsum("skgd,tkd->skgt", query_heads, cached_keys, preferred_element_type=jnp.float32)
        * scale_factor
    )
    own_score = (
        jnp.einsum("skgd,skd->skg", query_heads, key_new, preferred_element_type=jnp.float32)
        * scale_factor
    )
    token_pos = jnp.arange(pool_tokens, dtype=jnp.int32)
    inside = (token_pos[None, :] >= slot_offset[:, None]) & (
        token_pos[None, :] < (slot_offset + slot_length)[:, None]
    )
    inside = inside[:, None, None, :]
    largest = jnp.maximum(jnp.max(jnp.where(inside, scores, -1e30), axis=3), own_score)
    weights = jnp.where(inside, jnp.exp(scores - largest[..., None]), 0.0)
    own_weight = jnp.exp(own_score - largest)
    denominator = jnp.sum(weights, axis=3) + own_weight
    summed = jnp.einsum(
        "skgt,tkd->skgd",
        weights.astype(jnp.bfloat16),
        cached_values,
        preferred_element_type=jnp.float32,
    )
    own_low = own_weight.astype(jnp.bfloat16).astype(jnp.float32)
    summed = summed + own_low[..., None] * value_new.astype(jnp.float32)[:, :, None, :]
    head_out = (
        (summed / denominator[..., None])
        .astype(jnp.bfloat16)
        .reshape(slot_count, devices, query_cols)
    )
    returned = lax.all_to_all(head_out, ("pool", "tensor"), split_axis=1, concat_axis=0, tiled=True)
    head_rows = returned.reshape(devices * slot_count, query_cols)[request_slot]
    partial_value = jnp.dot(head_rows, output_weight, preferred_element_type=jnp.float32)
    row_start = device_index * local_rows
    own_part = lax.dynamic_slice_in_dim(partial_value, row_start, local_rows, 0) + hidden.astype(
        jnp.float32
    )
    partial_value = lax.dynamic_update_slice_in_dim(partial_value, own_part, row_start, 0)
    totals = lax.psum(partial_value, ("pool", "tensor"))
    mixed_all = totals.astype(jnp.bfloat16)
    mixed_rows = lax.dynamic_slice_in_dim(mixed_all, row_start, local_rows, 0)
    post_normed = rms_scale(mixed_all, post_gain).astype(jnp.bfloat16)
    gate_part = jnp.dot(post_normed, gate_weight, preferred_element_type=jnp.float32)
    up_part = jnp.dot(post_normed, up_weight, preferred_element_type=jnp.float32)
    activated = (jax.nn.silu(gate_part) * up_part).astype(jnp.bfloat16)
    lowered = lax.psum_scatter(
        jnp.dot(activated, down_weight, preferred_element_type=jnp.float32),
        ("pool", "tensor"),
        scatter_dimension=0,
        tiled=True,
    )
    final_rows = (mixed_rows.astype(jnp.float32) + lowered).astype(jnp.bfloat16)
    return (mixed_rows, final_rows)


MESH = pl.DeviceIdType.MESH
F32 = jnp.float32
BF16 = jnp.bfloat16
CUTS = 2


def step_kernel(
    pool,
    tensor,
    hidden_hbm,
    slot_hbm,
    length_hbm,
    input_gain_hbm,
    frequency_hbm,
    query_gain_hbm,
    key_gain_hbm,
    post_gain_hbm,
    qw_hbm,
    kw_hbm,
    vw_hbm,
    ow_hbm,
    gw_hbm,
    uw_hbm,
    dw_hbm,
    kc_hbm,
    vc_hbm,
    mixed_ref,
    added_ref,
    hidden_ref,
    slot_ref,
    length_ref,
    input_gain_ref,
    frequency_ref,
    query_gain_ref,
    key_gain_ref,
    post_gain_ref,
    qw,
    kvw,
    ow,
    gw,
    uw,
    dw,
    kc,
    vc,
    ag1,
    hid,
    hblock,
    xs,
    to_owner,
    at_owner,
    to_home,
    at_home,
    part1,
    peer1,
    out1,
    in1,
    mb,
    part2,
    peer2,
    sum2,
    out2,
    in2,
    small_sem,
    load_sem,
    ag1_s,
    ag1_r,
    hid_s,
    hid_r,
    ag2_s,
    ag2_r,
    a1_s,
    a1_r,
    a2_s,
    a2_r,
    sw1_s,
    sw1_r,
    rs1_s,
    rs1_r,
    sw2_s,
    sw2_r,
    rs2_s,
    rs2_r,
):
    devices = pool * tensor
    rows, width = hidden_ref.shape
    requests = devices * rows
    half = tensor * rows
    block = width // tensor
    head_dim = query_gain_ref.shape[1]
    query_cols = qw.shape[1]
    key_cols = kvw.shape[0] // 2
    heads_here = query_cols // head_dim
    head_count = devices * heads_here
    kv_count = devices * key_cols // head_dim
    per_kv = devices // kv_count
    group = head_count // kv_count
    hidden_units = gw.shape[0]
    pieces = heads_here + 2
    span = 2 * SLOTS
    p = lax.axis_index("pool")
    t = lax.axis_index("tensor")
    me = p * tensor + t
    partner = {"pool": 1 - p, "tensor": t}

    barrier = pltpu.get_barrier_semaphore()

    def place(index):
        return {"pool": lax.div(index, tensor), "tensor": lax.rem(index, tensor)}

    for j in range(1, devices):
        pl.semaphore_signal(
            barrier, inc=1, device_id=place(lax.rem(me + j, devices)), device_id_type=MESH
        )

    smalls = [
        pltpu.make_async_copy(a, b, small_sem.at[i])
        for i, (a, b) in enumerate(
            [
                (hidden_hbm, hidden_ref),
                (slot_hbm, slot_ref),
                (length_hbm, length_ref),
                (input_gain_hbm, input_gain_ref),
                (frequency_hbm, frequency_ref),
                (query_gain_hbm, query_gain_ref),
                (key_gain_hbm, key_gain_ref),
                (post_gain_hbm, post_gain_ref),
            ]
        )
    ]
    for load in smalls:
        load.start()

    loads = [
        pltpu.make_async_copy(a, b, load_sem.at[i])
        for i, (a, b) in enumerate(
            [
                (qw_hbm, qw),
                (kw_hbm, kvw.at[:key_cols]),
                (vw_hbm, kvw.at[key_cols:]),
                (kc_hbm, kc),
                (vc_hbm, vc),
                (ow_hbm, ow),
                (gw_hbm, gw),
                (uw_hbm, uw),
                (dw_hbm, dw),
            ]
        )
    ]

    def flip(j):
        out, bit = 0, 1
        while bit < tensor:
            digit = lax.rem(lax.div(t, bit), 2)
            out = out + bit * (1 - digit if (j // bit) % 2 else digit)
            bit *= 2
        return out

    around = range(1, tensor)
    spin = [lax.rem(t + j, tensor) for j in range(tensor)]
    if tensor == 8:
        deep, side = lax.div(t, 2), lax.rem(t, 2)
        upper = lax.div(deep, 2)
        layers = [deep, deep + 1 - 2 * lax.rem(deep, 2), 2 - upper, 3 - 3 * upper]
        near = [2 * layer + q for layer in layers for q in (side, 1 - side)]
    else:
        near = [flip(j) for j in range(tensor)]

    def remote(source, target, sent, received, where):
        return pltpu.make_async_remote_copy(
            src_ref=source,
            dst_ref=target,
            send_sem=sent,
            recv_sem=received,
            device_id=where,
            device_id_type=MESH,
        )

    def in_plane(other):
        return {"pool": p, "tensor": other}

    class Gather:
        def __init__(self, buffer, sent, received, order):
            self.buffer, self.sent, self.received, self.order = buffer, sent, received, order

        def slot(self, q, index, k, where):
            at = self.buffer.at[q, index]
            return remote(at, at, self.sent.at[k], self.received.at[q, index], where)

        def send(self):
            self.slot(p, t, 0, partner).start()
            for j in around:
                self.slot(p, t, j, in_plane(self.order[j])).start()

        def forward(self, j):
            self.slot(p, near[j], tensor + j, partner).wait_recv()
            self.slot(p, near[j], tensor + j, partner).start()

        def across(self, j):
            self.slot(1 - p, near[j], 0, partner).wait_recv()

        def finish(self):
            self.slot(p, t, 0, partner).wait_send()
            for j in around:
                self.slot(p, t, j, in_plane(self.order[j])).wait_send()
                self.slot(p, near[j], tensor + j, partner).wait_send()

    first = Gather(ag1, ag1_s, ag1_r, spin)
    second = Gather(mb, ag2_s, ag2_r, near)

    def hidden_copy(j, index):
        lanes = pl.ds(pl.multiple_of(near[j] * block, block), block)
        return remote(
            hidden_ref.at[:, lanes], hid.at[index], hid_s.at[j], hid_r.at[index], in_plane(near[j])
        )

    for load in smalls:
        load.wait()
    for load in loads:
        load.start()
    hidden = hidden_ref[...].astype(F32)
    ag1[p, t] = rms_scale(hidden, input_gain_ref[...]).astype(BF16)

    slot_row = slot_ref[...]
    length_row = length_ref[...]

    def iota(shape, dim):
        return lax.broadcasted_iota(jnp.int32, shape, dim)

    def hot(mask):
        return mask.astype(F32).astype(BF16)

    spread = hot(iota((requests, pieces * requests), 0) == lax.rem(iota((requests, pieces * requests), 1), requests))
    slot_wide = jnp.broadcast_to(slot_row, (span, requests))
    slot_tiled = jnp.dot(
        slot_wide.astype(F32).astype(BF16), spread, preferred_element_type=F32
    ).astype(jnp.int32)[:1]
    tall = devices * pieces * SLOTS
    row = iota((tall, pieces * requests), 0)
    col = iota((tall, pieces * requests), 1)
    wanted = lax.div(row, pieces * SLOTS) * SLOTS + lax.rem(row, SLOTS)
    scatter_hot = hot(
        (lax.rem(lax.div(row, SLOTS), pieces) == lax.div(col, requests)) & (wanted == slot_tiled)
    )
    eye = iota((requests, requests), 0) == iota((requests, requests), 1)
    slot_col = jnp.sum(
        jnp.where(eye, jnp.broadcast_to(slot_row, (requests, requests)), 0).astype(F32),
        axis=1,
        keepdims=True,
    ).astype(jnp.int32)
    home = devices * heads_here * SLOTS
    col = iota((requests, home), 1)
    held = lax.div(col, heads_here * SLOTS) * SLOTS + lax.rem(col, SLOTS)
    which = lax.rem(lax.div(col, SLOTS), heads_here)
    gather_hot = jnp.concatenate(
        [hot((which == i) & (held == slot_col)) for i in range(heads_here)], axis=0
    )
    place_id = lax.rem(iota((span, requests), 0), SLOTS)
    length_wide = jnp.broadcast_to(length_row, (span, requests)).astype(F32)
    base = me * SLOTS
    slot_length = jnp.sum(
        jnp.where(slot_wide == base + place_id, length_wide, 0.0), axis=1, keepdims=True
    )
    slot_offset = jnp.sum(
        jnp.where((slot_wide >= base) & (slot_wide < base + place_id), length_wide, 0.0),
        axis=1,
        keepdims=True,
    )
    angles = slot_length * frequency_ref[...]
    cosine = jnp.cos(angles)
    lane = iota((span, head_dim), 1)
    sine_part = jnp.where(lane < head_dim // 2, -jnp.sin(angles), jnp.sin(angles))
    pool_tokens = kc.shape[0]
    token = iota((span, pool_tokens), 1).astype(F32)
    inside = jnp.where((token >= slot_offset) & (token < slot_offset + slot_length), 1.0, 0.0)

    def turn(values, scale, copies):
        scaled = rms_scale(values, scale)
        return scaled * jnp.tile(cosine, (copies, 1)) + pltpu.roll(
            scaled, head_dim // 2, 1
        ) * jnp.tile(sine_part, (copies, 1))

    def turned(left, weight):
        return lax.dot_general(left, weight, (((1,), (1,)), ((), ())), preferred_element_type=F32)

    wide = iota((2 * key_cols, 2 * head_dim), 1)
    tall = iota((2 * key_cols, 2 * head_dim), 0)
    shift = lax.rem(me, per_kv) * key_cols
    aim = jnp.where(tall < key_cols, tall + shift, tall - key_cols + head_dim + shift)
    shift_hot = hot(aim == wide)
    pl.semaphore_wait(barrier, devices - 1)
    first.send()
    hid[t] = hidden_ref[:, pl.ds(pl.multiple_of(t * block, block), block)]
    for load in loads[:3]:
        load.wait()
    for j in around:
        first.forward(j)
    for j in around:
        hidden_copy(j, t).start()
    for index in range(tensor):
        xs[p, index * rows : (index + 1) * rows, :] = ag1[p, index]
    for j in range(tensor):
        first.across(j)
    for index in range(tensor):
        xs[1 - p, index * rows : (index + 1) * rows, :] = ag1[1 - p, index]

    left = jnp.concatenate([xs[q] for q in range(pool)], axis=0)
    query_part = jnp.dot(left, qw[...], preferred_element_type=F32).astype(BF16)
    kv_part = turned(left, kvw[...]).astype(BF16)

    kv_wide = jnp.dot(kv_part, shift_hot, preferred_element_type=F32).astype(BF16)
    stacked = jnp.concatenate(
        [query_part[:, i * head_dim : (i + 1) * head_dim] for i in range(heads_here)]
        + [kv_wide[:, :head_dim], kv_wide[:, head_dim:]],
        axis=0,
    )
    slots = jnp.dot(scatter_hot, stacked, preferred_element_type=F32).astype(BF16)
    deep = pieces * SLOTS
    for index in range(devices):
        to_owner[index] = slots[index * deep : (index + 1) * deep]

    own_group, own_seat = lax.div(me, per_kv), lax.rem(me, per_kv)
    side_groups = kv_count // pool
    depth = lax.rem(own_group, side_groups)
    turns = [(0, 0)] + [(q, h) for q in (0, 1) for h in range(1, side_groups)] + [(1, 0)]
    groups = [
        (p if q == 0 else 1 - p) * side_groups + lax.rem(depth + h, side_groups) for q, h in turns
    ]

    def members(g):
        if g == 0:
            return [(j, groups[0] * per_kv + lax.rem(own_seat + j, per_kv)) for j in range(1, per_kv)]
        return [
            (g * per_kv + j, groups[g] * per_kv + lax.rem(own_seat + j, per_kv))
            for j in range(per_kv)
        ]

    everyone = [member for g in range(kv_count) for member in members(g)]

    def post(outgoing, incoming, sent, received, number, peer):
        return remote(
            outgoing.at[peer], incoming.at[me], sent.at[number], received.at[me], place(peer)
        )

    def arrival(outgoing, incoming, sent, received, number, peer):
        return remote(
            outgoing.at[peer], incoming.at[peer], sent.at[number], received.at[peer], place(peer)
        )

    one = (to_owner, at_owner, a1_s, a1_r)
    two = (to_home, at_home, a2_s, a2_r)
    for member in everyone:
        post(*one, *member).start()
    at_owner[me] = to_owner[me]

    for j in around:
        hidden_copy(j, near[j]).wait_recv()
    for index in range(tensor):
        hblock[index * rows : (index + 1) * rows, :] = hid[index].astype(F32)
    for load in loads[3:5]:
        load.wait()

    scale_factor = 1.0 / math.sqrt(head_dim)
    copies = group * SLOTS // span
    allowed = jnp.tile(inside, (copies, 1)) > 0.5
    upper = iota((span, head_dim), 0) < SLOTS
    deep = heads_here * SLOTS
    for g in range(kv_count):
        for member in members(g):
            arrival(*one, *member).wait_recv()
        k = groups[g]
        blocks = [at_owner[k * per_kv + j].astype(F32) for j in range(per_kv)]
        query = jnp.concatenate([b[:deep] for b in blocks], axis=0)
        both = blocks[0][deep:]
        for b in blocks[1:]:
            both = both + b[deep:]
        turned_over = pltpu.roll(both, SLOTS, 0)
        key_new = turn(jnp.where(upper, both, turned_over), key_gain_ref[...], 1)
        own_value = jnp.tile(jnp.where(upper, turned_over, both), (copies, 1))
        own_key = jnp.tile(key_new.astype(BF16).astype(F32), (copies, 1))
        query = turn(query, query_gain_ref[...], copies).astype(BF16)
        lanes = pl.ds(pl.multiple_of(k * head_dim, head_dim), head_dim)
        scores = turned(query, kc[:, lanes]) * scale_factor
        own_score = jnp.sum(query.astype(F32) * own_key, axis=1, keepdims=True) * scale_factor
        scores = jnp.where(allowed, scores, -1e30)
        largest = jnp.maximum(jnp.max(scores, axis=1, keepdims=True), own_score)
        weights = jnp.exp(scores - largest)
        own_weight = jnp.exp(own_score - largest)
        denominator = jnp.sum(weights, axis=1, keepdims=True) + own_weight
        summed = jnp.dot(weights.astype(BF16), vc[:, lanes], preferred_element_type=F32)
        summed = summed + own_weight.astype(BF16).astype(F32) * own_value
        head_out = summed / denominator
        for j in range(per_kv):
            to_home[k * per_kv + j] = head_out[j * deep : (j + 1) * deep]
        for member in members(g):
            post(*two, *member).start()
    at_home[me] = to_home[me]

    loads[5].wait()
    for member in everyone:
        arrival(*two, *member).wait_recv()
    back = jnp.concatenate([at_home[index] for index in range(devices)], axis=0).astype(BF16)
    gathered = jnp.dot(gather_hot, back, preferred_element_type=F32).astype(BF16)
    head_rows = jnp.concatenate(
        [gathered[i * requests : (i + 1) * requests] for i in range(heads_here)], axis=1
    )

    pairs = tensor // 2
    wide = 2 * block

    def swap(part, peer, sent, received, c):
        return remote(part.at[c, 1 - p], peer.at[c], sent.at[c], received.at[c], partner)

    def products(left, weight, part, peer, sent, received, order):
        wide = part.shape[-1]
        for c in range(part.shape[0]):
            at = pl.ds(pl.multiple_of(order[c] * wide, wide), wide)
            product = jnp.dot(left, weight[:, at], preferred_element_type=F32)
            for q in range(pool):
                part[c, q] = product[q * half : (q + 1) * half].astype(BF16)
            swap(part, peer, sent, received, c).start()

    turn_of = [lax.rem(lax.div(t, 2) + 1 + c, pairs) for c in range(pairs)]
    products(head_rows, ow, part1, peer1, sw1_s, sw1_r, turn_of)

    def block_copy(k, other, slot):
        return remote(out1.at[other], in1.at[slot], rs1_s.at[k], rs1_r.at[slot], in_plane(other))

    for c in range(pairs):
        swap(part1, peer1, sw1_s, sw1_r, c).wait_recv()
        total = (peer1[c].astype(F32) + part1[c, p].astype(F32)).astype(BF16)
        for i in range(2):
            out1[2 * turn_of[c] + i] = total[:, i * block : (i + 1) * block]
        if c + 1 < pairs:
            for i in range(2):
                block_copy(2 * c + i, 2 * turn_of[c] + i, t).start()
    block_copy(tensor - 2, near[1], t).start()
    total = hblock[...] + out1[t].astype(F32)
    for j in around:
        block_copy(0, near[j], near[j]).wait_recv()
        total = total + in1[near[j]].astype(F32)
    mb[p, t] = total.astype(BF16)
    second.send()

    def part_of(j):
        at = pl.ds(pl.multiple_of(near[j] * block, block), block)
        values = jnp.concatenate([mb[q, near[j]] for q in range(pool)], axis=0).astype(F32)
        squares = values * values
        some = squares[:, :128]
        for i in range(1, block // 128):
            some = some + squares[:, i * 128 : (i + 1) * 128]
        scaled = (values * post_gain_ref[:, at]).astype(BF16)
        return some, turned(scaled, gw[:, at]), turned(scaled, uw[:, at])

    loads[6].wait()
    loads[7].wait()
    lead = 2
    sent_up_to = 0
    acc = None
    for j in range(tensor):
        while sent_up_to < min(j + lead, tensor - 1) and j > 0 or sent_up_to < j:
            sent_up_to += 1
            second.forward(sent_up_to)
        second.across(j)
        new = part_of(j)
        acc = new if acc is None else tuple(a + b for a, b in zip(acc, new))
    square, gate_part, up_part = acc
    mean = jnp.sum(square, axis=1, keepdims=True) * (1.0 / width)
    scale = lax.rsqrt(mean + eps)
    gate_part = gate_part * scale
    up_part = up_part * scale
    activated = (gate_part / (1.0 + jnp.exp(-gate_part)) * up_part).astype(BF16)

    loads[8].wait()
    cuts = part2.shape[0]
    wide = width // cuts
    products(activated, dw, part2, peer2, sw2_s, sw2_r, list(range(cuts)))

    def row_copy(j, slot):
        return remote(
            out2.at[spin[j]], in2.at[slot], rs2_s.at[j], rs2_r.at[slot], in_plane(spin[j])
        )

    for c in range(cuts):
        lanes = slice(c * wide, (c + 1) * wide)
        swap(part2, peer2, sw2_s, sw2_r, c).wait_recv()
        sum2[:, lanes] = peer2[c].astype(F32) + part2[c, p].astype(F32)
        for index in range(tensor):
            out2[index, :, lanes] = sum2[index * rows : (index + 1) * rows, lanes].astype(BF16)
    for j in around:
        row_copy(j, t).start()

    pick = hot(iota((8, requests), 1) == me * rows + iota((8, requests), 0))
    mixed_ref[...] = jnp.concatenate(
        [
            jnp.dot(
                pick,
                jnp.concatenate([mb[q, index] for q in range(pool)], axis=0),
                preferred_element_type=F32,
            )[:rows]
            for index in range(tensor)
        ],
        axis=1,
    )
    first.finish()
    for member in everyone:
        post(*one, *member).wait_send()
        post(*two, *member).wait_send()
    second.finish()
    for j in around:
        hidden_copy(j, t).wait_send()
    for c in range(pairs):
        swap(part1, peer1, sw1_s, sw1_r, c).wait_send()
    for c in range(cuts):
        swap(part2, peer2, sw2_s, sw2_r, c).wait_send()
    for c in range(pairs - 1):
        for i in range(2):
            block_copy(2 * c + i, 2 * turn_of[c] + i, t).wait_send()
    block_copy(tensor - 2, near[1], t).wait_send()

    total = out2[t].astype(F32)
    for j in around:
        row_copy(j, spin[j]).wait_recv()
        total = total + in2[spin[j]].astype(F32)
    added_ref[...] = total
    for j in around:
        row_copy(j, t).wait_send()


def fused(pool, tensor, *operands):
    (
        hidden,
        input_gain,
        query_weight,
        key_weight,
        value_weight,
        query_gain,
        key_gain,
        output_weight,
        post_gain,
        gate_weight,
        up_weight,
        down_weight,
        key_cache,
        value_cache,
        lengths,
        request_slot,
    ) = operands
    devices = pool * tensor
    rows, width = hidden.shape
    head_dim = query_gain.shape[0]
    query_cols = query_weight.shape[1]
    key_cols = key_weight.shape[1]
    heads_here = query_cols // head_dim
    half = tensor * rows
    block = width // tensor
    pairs = tensor // 2
    half_width = head_dim // 2
    frequency = theta ** (-np.arange(half_width) * 2.0 / head_dim)
    frequency = np.concatenate([frequency, frequency])[None, :].astype(np.float32)
    gate_turned, up_turned = gate_weight.T, up_weight.T
    dma = pltpu.SemaphoreType.DMA
    deep = (heads_here + 2) * SLOTS
    small = (
        hidden,
        request_slot[None, :],
        lengths[None, :],
        input_gain[None, :],
        frequency,
        query_gain[None, :],
        key_gain[None, :],
        post_gain[None, :],
    )
    scratch = [pltpu.VMEM(v.shape, v.dtype) for v in small] + [
        pltpu.VMEM(query_weight.shape, BF16),
        pltpu.VMEM((2 * key_cols, width), BF16),
        pltpu.VMEM(output_weight.shape, BF16),
        pltpu.VMEM(gate_turned.shape, BF16),
        pltpu.VMEM(up_turned.shape, BF16),
        pltpu.VMEM(down_weight.shape, BF16),
        pltpu.VMEM(key_cache.shape, BF16),
        pltpu.VMEM(value_cache.shape, BF16),
        pltpu.VMEM((pool, tensor, rows, width), BF16),
        pltpu.VMEM((tensor, rows, block), BF16),
        pltpu.VMEM((half, block), F32),
        pltpu.VMEM((pool, half, width), BF16),
        pltpu.VMEM((devices, deep, head_dim), BF16),
        pltpu.VMEM((devices, deep, head_dim), BF16),
        pltpu.VMEM((devices, heads_here * SLOTS, head_dim), F32),
        pltpu.VMEM((devices, heads_here * SLOTS, head_dim), F32),
        pltpu.VMEM((pairs, pool, half, 2 * block), BF16),
        pltpu.VMEM((pairs, half, 2 * block), BF16),
        pltpu.VMEM((tensor, half, block), BF16),
        pltpu.VMEM((tensor, half, block), BF16),
        pltpu.VMEM((pool, tensor, half, block), BF16),
        pltpu.VMEM((CUTS, pool, half, width // CUTS), BF16),
        pltpu.VMEM((CUTS, half, width // CUTS), BF16),
        pltpu.VMEM((half, width), F32),
        pltpu.VMEM((tensor, rows, width), BF16),
        pltpu.VMEM((tensor, rows, width), BF16),
        dma((len(small),)),
        dma((9,)),
        dma((2 * tensor,)),
        dma((pool, tensor)),
        dma((tensor,)),
        dma((tensor,)),
        dma((2 * tensor,)),
        dma((pool, tensor)),
        dma((devices,)),
        dma((devices,)),
        dma((devices,)),
        dma((devices,)),
        dma((pairs,)),
        dma((pairs,)),
        dma((tensor,)),
        dma((tensor,)),
        dma((CUTS,)),
        dma((CUTS,)),
        dma((tensor,)),
        dma((tensor,)),
    ]
    vmem = pl.BlockSpec(memory_space=pltpu.VMEM)
    hbm = pl.BlockSpec(memory_space=pl.ANY)
    row = pltpu.VMEM(hidden.shape, F32)
    mixed, added = pl.pallas_call(
        functools.partial(step_kernel, pool, tensor),
        out_shape=(row, row),
        in_specs=[hbm] * (len(small) + 9),
        out_specs=(vmem, vmem),
        scratch_shapes=scratch,
        compiler_params=pltpu.CompilerParams(
            collective_id=0, has_side_effects=True, vmem_limit_bytes=62 * 1024 * 1024
        ),
    )(
        *small,
        query_weight,
        key_weight.T,
        value_weight.T,
        output_weight,
        gate_turned,
        up_turned,
        down_weight,
        key_cache,
        value_cache,
    )
    return mixed.astype(hidden.dtype), (mixed + added).astype(hidden.dtype)


def dispatch(pool, tensor, *operands):
    rows, width = operands[0].shape
    query_cols = operands[2].shape[1]
    key_cols = operands[3].shape[1]
    head_dim = operands[5].shape[0]
    devices = pool * tensor
    lanes = width % (tensor * 128) == 0 and head_dim == 128
    paired = tensor >= 4 and tensor & (tensor - 1) == 0 and tensor * rows == 16
    heads = query_cols == 2 * head_dim and head_dim % key_cols == 0
    few = devices * SLOTS <= 256 and devices * rows * 4 % 128 == 0
    if pool == 2 and lanes and paired and heads and few:
        return fused(pool, tensor, *operands)
    return on_device(*operands)


def solution(mesh):
    placed = (
        P(("groups", "pool", "tensor"), None),
        P(),
        P(None, ("pool", "tensor")),
        P(None, ("pool", "tensor")),
        P(None, ("pool", "tensor")),
        P(),
        P(),
        P(("pool", "tensor"), None),
        P(),
        P(None, ("pool", "tensor")),
        P(None, ("pool", "tensor")),
        P(("pool", "tensor"), None),
        P(("groups", "pool", "tensor"), None),
        P(("groups", "pool", "tensor"), None),
        P("groups"),
        P("groups"),
    )
    return jax.shard_map(
        functools.partial(dispatch, mesh.shape["pool"], mesh.shape["tensor"]),
        mesh=mesh,
        in_specs=placed,
        out_specs=(P(("groups", "pool", "tensor"), None), P(("groups", "pool", "tensor"), None)),
        check_vma=False,
    )
```
